512 devices in a mesh: seq: 64 (over x, z, core), blk: 8 (over y).
Axes of the slice: x: 4, y: 8, z: 8, core: 2. Of those that a mesh axis runs over, the one named last changes fastest.
Arguments:
- query_states: bfloat16 [65536, 2048], P(('seq', 'blk')), may hold values from -6 to 6
- key_states: bfloat16 [65536, 2048], P(('seq', 'blk')), may hold values from -6 to 6
- value_states: bfloat16 [65536, 2048], P(('seq', 'blk')), may hold values from -6 to 6
- output_grad: bfloat16 [65536, 2048], P(('seq', 'blk')), may hold values from -6 to 6
- near_mask: int32 [512, 2], replicated, may hold values 0 or 1
- motion_count: int32 [512], replicated, may hold values from 0 to 3
Outputs:
- query_grad: bfloat16 [65536, 2048], P(('seq', 'blk'))
- key_grad: bfloat16 [65536, 2048], P(('seq', 'blk'))
- value_grad: bfloat16 [65536, 2048], P(('seq', 'blk'))
The draws below stay inside these ranges and needn't reach their ends.
All inputs are finite; a program needn't handle non-finite values.
Results may differ from the reference program's by a relative error of at most 0.012.
Values may be sent and summed in bfloat16 or wider, within the bound.
No kernel may reach another device: no remote copies, remote signals or barrier semaphores. Data moves between devices by JAX's collectives and lax.ppermute only.
A program may use at most 64 MiB of HBM per device.

```python
from functools import partial
import jax
import jax.numpy as jnp
from jax import lax

HEADS = 32
HEAD_DIM = 64
TILE = 128
REACH = 2
TOKENS = 65536
QTILES = 512


def draw_query_states(key, part):
    shape_full = (TOKENS, HEADS * HEAD_DIM)
    result = jnp.clip(jax.random.normal(jax.random.fold_in(key, 1), shape_full, jnp.float32), -4.0, 4.0)
    return result.astype(jnp.bfloat16)


def draw_key_states(key, part):
    shape_full = (TOKENS, HEADS * HEAD_DIM)
    result = jnp.clip(jax.random.normal(jax.random.fold_in(key, 2), shape_full, jnp.float32), -4.0, 4.0)
    return result.astype(jnp.bfloat16)


def place_ends(values, rng, low, largest):
    longest = values.shape.index(max(values.shape))
    spots = []
    for shift in (0, 1):
        where = [jax.random.randint(jax.random.fold_in(rng, axis), (), 0, length) for axis, length in enumerate(values.shape)]
        where[longest] = (where[longest] + shift) % values.shape[longest]
        spots.append(tuple(where))
    return values.at[spots[0]].set(low).at[spots[1]].set(largest)


def levels(key, shape, shards, smallest, high):
    factor_of, own = 1.0, jax.random.fold_in(key, 6)
    for axis_at, shards_of in shards:
        heights = jnp.exp(jax.random.uniform(jax.random.fold_in(own, axis_at), (shards_of,), jnp.float32, smallest / len(shards), high / len(shards)))
        factor_of = factor_of * jnp.repeat(heights, shape[axis_at] // shards_of).reshape([-1 if axis == axis_at else 1 for axis in range(len(shape))])
    return factor_of


def gaussian(key, dims, scale, most, shards=(), kind=jnp.bfloat16):
    entries = scale * jax.random.normal(key, dims, jnp.float32)
    if shards:
        entries = entries * levels(key, dims, shards, -0.22, 0.18)
    return jnp.clip(entries, -most, most).astype(kind)


def setup_inputs(seed: int = 0) -> dict:
    splits = jax.random.split(jax.random.key(seed), 7)
    return {
        "query_states": draw_query_states(jax.random.fold_in(splits[6], 71), 0),
        "key_states": draw_key_states(jax.random.fold_in(splits[6], 71), 0),
        "value_states": gaussian(splits[2], (TOKENS, HEADS * HEAD_DIM), 1.0, 6.0, ((0, 512),)),
        "output_grad": gaussian(splits[3], (TOKENS, HEADS * HEAD_DIM), 1.0, 6.0, ((0, 512),)),
        "near_mask": place_ends((jax.random.randint(splits[4], (QTILES, 2), 0, 4) < 3).astype(jnp.int32), jax.random.fold_in(splits[4], 1), 0, 1),
        "motion_count": place_ends(jax.random.randint(splits[5], (QTILES,), 0, 4), jax.random.fold_in(splits[5], 1), 0, 3).astype(jnp.int32),
    }


def tile_allow(mask_rows, motion_rows, query_tile0, key_tile0, tiles_all, query_tiles, key_tiles, tile_size):
    query_ids = query_tile0 + jnp.arange(query_tiles, dtype=jnp.int32)[:, None]
    key_ids = key_tile0 + jnp.arange(key_tiles, dtype=jnp.int32)[None, :]
    spread = key_ids - query_ids
    near = (spread == 0) | (spread == -1) & (mask_rows[:, 0:1] == 1) | (spread == 1) & (mask_rows[:, 1:2] == 1)
    far_ok = (jnp.abs(spread) >= 2) & (jnp.abs(spread) <= REACH) & (motion_rows[:, None] >= 2)
    inside = (key_ids >= 0) & (key_ids < tiles_all)
    tile_ok = (near | far_ok) & inside
    spread_out = jnp.broadcast_to(tile_ok[:, None, :, None], (query_tiles, tile_size, key_tiles, tile_size))
    return spread_out.reshape(query_tiles * tile_size, key_tiles * tile_size)

def block_grad(query_rows, key_rows, value_rows, grad_rows, allowed, scale_factor):
    query_wide = query_rows.astype(jnp.float32)
    key_wide = key_rows.astype(jnp.float32)
    value_wide = value_rows.astype(jnp.float32)
    grad_wide = grad_rows.astype(jnp.float32)
    scores = jnp.dot(query_wide, key_wide.T, preferred_element_type=jnp.float32) * scale_factor
    scores = jnp.where(allowed, scores, -1e+30)
    row_max = lax.optimization_barrier(jnp.max(scores, axis=1, keepdims=True))
    weights_raw = jnp.exp(scores - row_max)
    probs = weights_raw / lax.optimization_barrier(jnp.sum(weights_raw, axis=1, keepdims=True))
    probs_b = probs.astype(jnp.bfloat16)
    probs_wide = probs_b.astype(jnp.float32)
    attn_out = jnp.dot(probs_wide, value_wide, preferred_element_type=jnp.float32)
    delta = lax.optimization_barrier(jnp.sum(grad_wide * attn_out, axis=1, keepdims=True))
    dprobs = jnp.dot(grad_wide, value_wide.T, preferred_element_type=jnp.float32)
    dscores = (probs * (dprobs - delta)).astype(jnp.bfloat16)
    dscores_wide = dscores.astype(jnp.float32)
    query_part = jnp.dot(dscores_wide, key_wide, preferred_element_type=jnp.float32) * scale_factor
    key_part = jnp.dot(dscores_wide.T, query_wide, preferred_element_type=jnp.float32) * scale_factor
    value_part = jnp.dot(probs_wide.T, grad_wide, preferred_element_type=jnp.float32)
    return (query_part, key_part, value_part)

def reference(query_states, key_states, value_states, output_grad, near_mask, motion_count):
    span = REACH * TILE
    blocks = TOKENS // span
    scale_factor = float(HEAD_DIM) ** (-0.5)
    queries = query_states.reshape(TOKENS, HEADS, HEAD_DIM)
    grads_in = output_grad.reshape(TOKENS, HEADS, HEAD_DIM)
    padding = ((span, span), (0, 0), (0, 0))
    keys_pad = jnp.pad(key_states.reshape(TOKENS, HEADS, HEAD_DIM), padding)
    values_pad = jnp.pad(value_states.reshape(TOKENS, HEADS, HEAD_DIM), padding)
    per_head = jax.vmap(partial(block_grad, scale_factor=scale_factor), in_axes=(1, 1, 1, 1, None), out_axes=1)
    zeros_block = jnp.zeros((2, span, HEADS, HEAD_DIM), jnp.float32)

    def step_block(running, block_index):
        pending_prev, pending_now = running
        row_start = block_index * span
        query_rows = lax.dynamic_slice_in_dim(queries, row_start, span, 0)
        grad_rows = lax.dynamic_slice_in_dim(grads_in, row_start, span, 0)
        key_rows = lax.dynamic_slice_in_dim(keys_pad, row_start, 3 * span, 0)
        value_rows = lax.dynamic_slice_in_dim(values_pad, row_start, 3 * span, 0)
        query_tile0 = (row_start // TILE).astype(jnp.int32)
        mask_rows = lax.dynamic_slice_in_dim(near_mask, query_tile0, span // TILE, 0)
        motion_rows = lax.dynamic_slice_in_dim(motion_count, query_tile0, span // TILE, 0)
        allowed = tile_allow(mask_rows, motion_rows, query_tile0, query_tile0 - REACH, QTILES, span // TILE, 3 * span // TILE, TILE)
        query_part, key_part, value_part = per_head(query_rows, key_rows, value_rows, grad_rows, allowed)
        both = jnp.stack([key_part, value_part])
        finished = pending_prev + both[:, 0:span]
        new_prev = pending_now + both[:, span:2 * span]
        new_now = both[:, 2 * span:3 * span]
        return ((new_prev, new_now), (query_part.astype(jnp.bfloat16), finished.astype(jnp.bfloat16)))
    indices = jnp.arange(blocks, dtype=jnp.int32)
    (last_prev, last_now), (query_blocks, done_blocks) = lax.scan(step_block, (zeros_block, zeros_block), indices)
    query_grad = query_blocks.reshape(TOKENS, HEADS * HEAD_DIM)
    tail = last_prev.astype(jnp.bfloat16)[None]
    kv_blocks = jnp.concatenate([done_blocks[1:], tail], axis=0)
    key_grad = kv_blocks[:, 0].reshape(TOKENS, HEADS * HEAD_DIM)
    value_grad = kv_blocks[:, 1].reshape(TOKENS, HEADS * HEAD_DIM)
    return (query_grad, key_grad, value_grad)
```

```python
import jax
import jax.numpy as jnp
from jax import lax
from jax.experimental import pallas as pl
from jax.experimental.pallas import tpu as pltpu
from jax.sharding import PartitionSpec as P

HEAD_DIM = 64
TILE = 128
REACH = 2
LANES = 128
CHUNKS = 2
WINDOW = 2 * REACH + 1


def cost(flops, moved, exps=0):
    return pl.CostEstimate(flops=flops, bytes_accessed=moved, transcendentals=exps)


def pack_body(q_ref, k_ref, v_ref, g_ref, out_ref):
    out_ref[0, 0] = q_ref[...]
    out_ref[0, 1] = k_ref[...]
    out_ref[0, 2] = v_ref[...]
    out_ref[0, 3] = g_ref[...]


def pack(arrays, chunk, peers):
    rows = arrays[0].shape[0]
    spec = pl.BlockSpec((rows, LANES), lambda b: (0, chunk * peers + b))
    return pl.pallas_call(
        pack_body,
        grid=(peers,),
        in_specs=[spec] * 4,
        out_specs=pl.BlockSpec((1, 4, rows, LANES), lambda b: (b, 0, 0, 0)),
        out_shape=jax.ShapeDtypeStruct((peers, 4, rows, LANES), jnp.bfloat16),
        cost_estimate=cost(0, 2 * peers * 4 * rows * LANES * 2),
        name="pack",
    )(*arrays)


def unpack_body(in_ref, *refs):
    outs = refs[-3:]
    for n in range(3):
        outs[n][...] = in_ref[0, n]


def unpack(grads, chunk, columns, so_far=None):
    peers, _, rows, _ = grads.shape
    spec = pl.BlockSpec((rows, LANES), lambda b: (0, chunk * peers + b))
    held = [] if so_far is None else list(so_far)
    return pl.pallas_call(
        unpack_body,
        grid=(peers,),
        in_specs=[pl.BlockSpec((1, 3, rows, LANES), lambda b: (b, 0, 0, 0))]
        + [pl.BlockSpec(memory_space=pl.ANY)] * len(held),
        out_specs=[spec] * 3,
        out_shape=[jax.ShapeDtypeStruct((rows, columns), jnp.bfloat16)] * 3,
        input_output_aliases={1 + n: n for n in range(len(held))},
        cost_estimate=cost(0, 2 * peers * 3 * rows * LANES * 2),
        name="unpack",
    )(grads, *held)


def attend_body(bias_ref, x_ref, left_ref, right_ref, out_ref, edge_ref, to_left_ref, to_right_ref,
                key_ref, value_ref, dkey_ref, dvalue_ref):
    tiles = x_ref.shape[0]
    span = WINDOW * TILE
    for n, ref in ((0, key_ref), (1, value_ref)):
        for t in range(REACH):
            ref[t * TILE:(t + 1) * TILE] = left_ref[t, n]
            at = (REACH + tiles + t) * TILE
            ref[at:at + TILE] = right_ref[t, n]
        for t in range(tiles):
            ref[(REACH + t) * TILE:(REACH + t + 1) * TILE] = x_ref[t, 1 + n]
    dkey_ref[...] = jnp.zeros_like(dkey_ref)
    dvalue_ref[...] = jnp.zeros_like(dvalue_ref)
    lane = lax.broadcasted_iota(jnp.int32, (TILE, LANES), 1)
    first = lane < HEAD_DIM
    scale = float(HEAD_DIM) ** (-0.5)

    def both_heads(block):
        zero = jnp.zeros_like(block)
        return jnp.concatenate([jnp.where(first, block, zero), jnp.where(first, zero, block)], axis=0)

    def step(i):
        at = pl.multiple_of(i * TILE, TILE)
        query = both_heads(x_ref[i, 0] * jnp.bfloat16(scale))
        grad = both_heads(x_ref[i, 3])
        key = key_ref[pl.ds(at, span)]
        value = value_ref[pl.ds(at, span)]
        nt = (((1,), (1,)), ((), ()))
        scores = lax.dot_general(key, query, nt, preferred_element_type=jnp.float32)
        scores = jnp.concatenate(
            [scores[t * TILE:(t + 1) * TILE] + bias_ref[i * WINDOW + t] for t in range(WINDOW)], axis=0)
        top = jnp.max(scores, axis=0, keepdims=True)
        weights = jnp.exp(scores - top)
        probs = weights * (1.0 / jnp.sum(weights, axis=0, keepdims=True))
        probs_b = probs.astype(jnp.bfloat16)
        dprobs = lax.dot_general(value, grad, nt, preferred_element_type=jnp.float32)
        delta = jnp.sum(probs_b.astype(jnp.float32) * dprobs, axis=0, keepdims=True)
        dscores = (probs * (dprobs - delta)).astype(jnp.bfloat16)
        dkey_ref[pl.ds(at, span)] += jnp.dot(dscores, query, preferred_element_type=jnp.float32)
        dvalue_ref[pl.ds(at, span)] += jnp.dot(probs_b, grad, preferred_element_type=jnp.float32)
        dquery = lax.dot_general(dscores, key, (((0,), (0,)), ((), ())), preferred_element_type=jnp.float32)
        out_ref[i, 0] = (jnp.where(first, dquery[:TILE], dquery[TILE:]) * scale).astype(jnp.bfloat16)

    def steps(i, _):
        step(2 * i)
        step(2 * i + 1)
        return 0

    lax.fori_loop(0, tiles // 2, steps, 0)
    for n, ref in ((0, dkey_ref), (1, dvalue_ref)):
        for t in range(REACH):
            to_left_ref[t, n] = ref[t * TILE:(t + 1) * TILE].astype(jnp.bfloat16)
            at = (REACH + tiles + t) * TILE
            to_right_ref[t, n] = ref[at:at + TILE].astype(jnp.bfloat16)
        for t in range(tiles):
            block = ref[(REACH + t) * TILE:(REACH + t + 1) * TILE]
            out_ref[t, 1 + n] = block.astype(jnp.bfloat16)
            if t < REACH or t >= tiles - REACH:
                edge_ref[t if t < REACH else t - tiles + 2 * REACH, n] = block


def attend(bias, taken, left, right):
    tiles = taken.shape[0]
    wide = (tiles + 2 * REACH) * TILE
    vmem = pl.BlockSpec(memory_space=pltpu.VMEM)
    pairs = tiles * WINDOW * 2
    return pl.pallas_call(
        attend_body,
        in_specs=[pl.BlockSpec(memory_space=pltpu.SMEM), vmem, vmem, vmem],
        out_specs=[vmem] * 4,
        out_shape=[
            jax.ShapeDtypeStruct((tiles, 3, TILE, LANES), jnp.bfloat16),
            jax.ShapeDtypeStruct((2 * REACH, 2, TILE, LANES), jnp.float32),
            jax.ShapeDtypeStruct((REACH, 2, TILE, LANES), jnp.bfloat16),
            jax.ShapeDtypeStruct((REACH, 2, TILE, LANES), jnp.bfloat16),
        ],
        scratch_shapes=[pltpu.VMEM((wide, LANES), jnp.bfloat16)] * 2 + [pltpu.VMEM((wide, LANES), jnp.float32)] * 2,
        cost_estimate=cost(pairs * 5 * 2 * TILE * TILE * HEAD_DIM * 8, 3 << 20, pairs * TILE * TILE),
        name="attend",
    )(bias, taken, left, right)


def edges_body(edge_ref, before_ref, after_ref, held_ref, out_ref):
    partial = jnp.where(pl.program_id(0) < REACH, before_ref[0, 0].astype(jnp.float32), after_ref[0, 0].astype(jnp.float32))
    out_ref[0, 0] = (edge_ref[0, 0] + partial).astype(jnp.bfloat16)


def add_edges(out, edge, before, after):
    tiles = out.shape[0]
    block = (1, 1, TILE, LANES)
    return pl.pallas_call(
        edges_body,
        grid=(2 * REACH, 2),
        in_specs=[
            pl.BlockSpec(block, lambda t, n: (t, n, 0, 0)),
            pl.BlockSpec(block, lambda t, n: (t % REACH, n, 0, 0)),
            pl.BlockSpec(block, lambda t, n: (t % REACH, n, 0, 0)),
            pl.BlockSpec(memory_space=pl.ANY),
        ],
        out_specs=pl.BlockSpec(
            block, lambda t, n: (t + (t // REACH) * (tiles - 2 * REACH), 1 + n, 0, 0)),
        out_shape=jax.ShapeDtypeStruct(out.shape, out.dtype),
        input_output_aliases={3: 0},
        cost_estimate=cost(1 << 17, 1 << 20),
        name="add_edges",
    )(edge, before, after, out)


def tile_bias(near_mask, motion_count, tiles):
    first = lax.axis_index("seq") * tiles
    near = lax.dynamic_slice_in_dim(near_mask, first, tiles, 0) == 1
    far = lax.dynamic_slice_in_dim(motion_count, first, tiles, 0) >= REACH
    index = first + jnp.arange(tiles)
    own = jnp.ones((tiles,), bool)
    allowed = jnp.stack([far, near[:, 0], own, near[:, 1], far], axis=1)
    others = index[:, None] + jnp.arange(-REACH, REACH + 1)[None, :]
    allowed &= (others >= 0) & (others < near_mask.shape[0])
    return jnp.where(allowed, 0.0, -1e30).astype(jnp.float32).reshape(-1)


def per_device(query_states, key_states, value_states, output_grad, near_mask, motion_count):
    peers, groups = lax.axis_size("blk"), lax.axis_size("seq")
    up = [(i, i + 1) for i in range(groups - 1)]
    down = [(j, i) for i, j in up]
    arrays = (query_states, key_states, value_states, output_grad)
    bias = tile_bias(near_mask, motion_count, peers)

    taken = [
        lax.all_to_all(pack(arrays, c, peers), "blk", split_axis=0, concat_axis=0, tiled=True)
        for c in range(CHUNKS)
    ]
    results = None
    for c in range(CHUNKS):
        left = lax.ppermute(taken[c][peers - REACH:, 1:3], "seq", up)
        right = lax.ppermute(taken[c][:REACH, 1:3], "seq", down)
        out, edge, to_left, to_right = attend(bias, taken[c], left, right)
        before = lax.ppermute(to_right, "seq", up)
        after = lax.ppermute(to_left, "seq", down)
        out = add_edges(out, edge, before, after)
        back = lax.all_to_all(out, "blk", split_axis=0, concat_axis=0, tiled=True)
        results = unpack(back, c, query_states.shape[1], results)
    return tuple(results)


def solution(mesh):
    spec = P(("seq", "blk"), None)
    return jax.shard_map(
        per_device, mesh=mesh, in_specs=(spec,) * 4 + (P(), P()), out_specs=(spec,) * 3, check_vma=False
    )
```

```python
import jax
import jax.numpy as jnp
from jax import lax
from jax.experimental import pallas as pl
from jax.experimental.pallas import tpu as pltpu
from jax.sharding import PartitionSpec as P


HEAD_DIM = 64
TILE = 128
REACH = 2
LANES = 128
CHUNKS = 2
WINDOW = 2 * REACH + 1
SPAN = WINDOW * TILE
NT = (((1,), (1,)), ((), ()))
TN = (((0,), (0,)), ((), ()))


def cost(flops, moved, exps=0):
    return pl.CostEstimate(flops=flops, bytes_accessed=moved, transcendentals=exps)


def pack(arrays, chunk, peers, after=()):
    rows, count = arrays[0].shape[0], len(arrays)

    def body(*refs):
        ins, refs = refs[:count], refs[count + len(after):]
        out_ref, held, in_sem, out_sem = refs
        reads = [
            [
                pltpu.make_async_copy(
                    ins[n].at[:, pl.ds((chunk * peers + b) * LANES, LANES)], held.at[b, n], in_sem.at[b, n])
                for n in range(count)
            ]
            for b in range(peers)
        ]
        writes = [pltpu.make_async_copy(held.at[b], out_ref.at[b], out_sem.at[b]) for b in range(peers)]
        for b in range(peers):
            for n in range(count):
                reads[b][n].start()
        for b in range(peers):
            for n in range(count):
                reads[b][n].wait()
            writes[b].start()
        for b in range(peers):
            writes[b].wait()

    shape = (peers, count, rows, LANES)
    return pl.pallas_call(
        body,
        in_specs=[pl.BlockSpec(memory_space=pl.ANY)] * (count + len(after)),
        out_specs=pl.BlockSpec(memory_space=pl.ANY),
        out_shape=jax.ShapeDtypeStruct(shape, jnp.bfloat16),
        scratch_shapes=[
            pltpu.VMEM(shape, jnp.bfloat16),
            pltpu.SemaphoreType.DMA((peers, count)),
            pltpu.SemaphoreType.DMA((peers,)),
        ],
        cost_estimate=cost(0, 2 * peers * count * rows * LANES * 2),
        name="pack",
    )(*arrays, *after)


def unpack(grads, chunk, columns, so_far=None):
    peers, count, rows, _ = grads.shape
    given = [] if so_far is None else list(so_far)

    def body(in_ref, *refs):
        outs = refs[len(given):len(given) + count]
        held, in_sem, out_sem = refs[len(given) + count:]
        reads = [pltpu.make_async_copy(in_ref.at[b], held.at[b], in_sem.at[b]) for b in range(peers)]
        writes = [
            [
                pltpu.make_async_copy(
                    held.at[b, n], outs[n].at[:, pl.ds((chunk * peers + b) * LANES, LANES)], out_sem.at[b, n])
                for n in range(count)
            ]
            for b in range(peers)
        ]
        for b in range(peers):
            reads[b].start()
        for b in range(peers):
            reads[b].wait()
            for n in range(count):
                writes[b][n].start()
        for b in range(peers):
            for n in range(count):
                writes[b][n].wait()

    hbm = pl.BlockSpec(memory_space=pl.ANY)
    return pl.pallas_call(
        body,
        in_specs=[hbm] * (1 + len(given)),
        out_specs=[hbm] * count,
        out_shape=[jax.ShapeDtypeStruct((rows, columns), jnp.bfloat16)] * count,
        scratch_shapes=[
            pltpu.VMEM(grads.shape, jnp.bfloat16),
            pltpu.SemaphoreType.DMA((peers,)),
            pltpu.SemaphoreType.DMA((peers, count)),
        ],
        input_output_aliases={1 + n: n for n in range(len(given))},
        compiler_params=pltpu.CompilerParams(vmem_limit_bytes=4 << 20),
        cost_estimate=cost(0, 2 * peers * count * rows * LANES * 2),
        name="unpack",
    )(grads, *given)


def rim_body(x_ref, low_ref, high_ref):
    tiles = x_ref.shape[0]
    deep = 2 * REACH
    for ref, wide, narrow in ((low_ref, 0, 0), (high_ref, tiles - deep, tiles - REACH)):
        for t in range(deep):
            ref[t] = x_ref[wide + t, 1]
            ref[deep + t] = x_ref[wide + t, 2]
        for t in range(REACH):
            ref[2 * deep + t] = x_ref[narrow + t, 0]
            ref[2 * deep + REACH + t] = x_ref[narrow + t, 3]


def rims(taken):
    shape = jax.ShapeDtypeStruct((6 * REACH,) + taken.shape[2:], taken.dtype)
    vmem = pl.BlockSpec(memory_space=pltpu.VMEM)
    return pl.pallas_call(
        rim_body,
        in_specs=[vmem],
        out_specs=[vmem] * 2,
        out_shape=[shape] * 2,
        compiler_params=pltpu.CompilerParams(vmem_limit_bytes=8 << 20),
        cost_estimate=cost(0, 2 << 20),
        name="rims",
    )(taken)


def attend_body(bias_ref, x_ref, left_ref, right_ref, out_ref, key_ref, value_ref, dkey_ref, dvalue_ref):
    tiles = x_ref.shape[0]
    deep = 2 * REACH
    for n, ref in ((0, key_ref), (1, value_ref)):
        for t in range(deep):
            ref[t * TILE:(t + 1) * TILE] = left_ref[n * deep + t]
            at = (deep + tiles + t) * TILE
            ref[at:at + TILE] = right_ref[n * deep + t]
        for t in range(tiles):
            ref[(deep + t) * TILE:(deep + t + 1) * TILE] = x_ref[t, 1 + n]
    dkey_ref[...] = jnp.zeros_like(dkey_ref)
    dvalue_ref[...] = jnp.zeros_like(dvalue_ref)
    first = lax.broadcasted_iota(jnp.int32, (TILE, LANES), 1) < HEAD_DIM
    scale = float(HEAD_DIM) ** (-0.5)

    def both_heads(block):
        zero = jnp.zeros_like(block)
        return jnp.concatenate([jnp.where(first, block, zero), jnp.where(first, zero, block)], axis=0)

    def scores_of(i, query_tile, grad_tile):
        at = i * TILE if isinstance(i, int) else pl.multiple_of(i * TILE, TILE)
        query = both_heads(query_tile * jnp.bfloat16(scale))
        grad = both_heads(grad_tile)
        key = key_ref[pl.ds(at, SPAN)]
        value = value_ref[pl.ds(at, SPAN)]
        scores = lax.dot_general(key, query, NT, preferred_element_type=jnp.float32)
        scores = jnp.concatenate(
            [scores[t * TILE:(t + 1) * TILE] + bias_ref[i * WINDOW + t] for t in range(WINDOW)], axis=0)
        top = jnp.max(scores, axis=0, keepdims=True)
        weights = jnp.exp(scores - top)
        probs = weights * (1.0 / jnp.sum(weights, axis=0, keepdims=True))
        probs_b = probs.astype(jnp.bfloat16)
        dprobs = lax.dot_general(value, grad, NT, preferred_element_type=jnp.float32)
        delta = jnp.sum(probs_b.astype(jnp.float32) * dprobs, axis=0, keepdims=True)
        return query, grad, key, probs, probs_b, dprobs, delta

    def near(i, query_tile, grad_tile):
        query, grad, _, probs, probs_b, dprobs, delta = scores_of(i, query_tile, grad_tile)
        low, high = max(0, deep - i), min(WINDOW, deep + tiles - i)
        rows = slice(low * TILE, high * TILE)
        dscores = (probs[rows] * (dprobs[rows] - delta)).astype(jnp.bfloat16)
        at = slice((i + low - REACH) * TILE, (i + high - REACH) * TILE)
        dkey_ref[at] += jnp.dot(dscores, query, preferred_element_type=jnp.float32)
        dvalue_ref[at] += jnp.dot(probs_b[rows], grad, preferred_element_type=jnp.float32)

    def step(t):
        query, grad, key, probs, probs_b, dprobs, delta = scores_of(t + REACH, x_ref[t, 0], x_ref[t, 3])
        dscores = (probs * (dprobs - delta)).astype(jnp.bfloat16)
        at = pl.multiple_of(t * TILE, TILE)
        dkey_ref[pl.ds(at, SPAN)] += jnp.dot(dscores, query, preferred_element_type=jnp.float32)
        dvalue_ref[pl.ds(at, SPAN)] += jnp.dot(probs_b, grad, preferred_element_type=jnp.float32)
        dquery = lax.dot_general(dscores, key, TN, preferred_element_type=jnp.float32)
        out_ref[t, 0] = (jnp.where(first, dquery[:TILE], dquery[TILE:]) * scale).astype(jnp.bfloat16)

    def steps(i, _):
        step(2 * i)
        step(2 * i + 1)
        return 0

    lax.fori_loop(0, tiles // 2, steps, 0)
    for t in range(REACH):
        near(t, left_ref[2 * deep + t], left_ref[2 * deep + REACH + t])
        near(REACH + tiles + t, right_ref[2 * deep + t], right_ref[2 * deep + REACH + t])
    for n, ref in ((0, dkey_ref), (1, dvalue_ref)):
        for t in range(tiles):
            out_ref[t, 1 + n] = ref[(REACH + t) * TILE:(REACH + t + 1) * TILE].astype(jnp.bfloat16)


def attend(bias, taken, left, right):
    tiles = taken.shape[0]
    wide = (tiles + 4 * REACH) * TILE
    vmem = pl.BlockSpec(memory_space=pltpu.VMEM)
    pairs = (tiles + 2 * REACH) * WINDOW * 2
    return pl.pallas_call(
        attend_body,
        in_specs=[pl.BlockSpec(memory_space=pltpu.SMEM), vmem, vmem, vmem],
        out_specs=vmem,
        out_shape=jax.ShapeDtypeStruct((tiles, 3, TILE, LANES), jnp.bfloat16),
        scratch_shapes=[pltpu.VMEM((wide, LANES), jnp.bfloat16)] * 2
        + [pltpu.VMEM(((tiles + 2 * REACH) * TILE, LANES), jnp.float32)] * 2,
        compiler_params=pltpu.CompilerParams(vmem_limit_bytes=32 << 20),
        cost_estimate=cost(pairs * 5 * 2 * TILE * TILE * HEAD_DIM * 8, 3 << 20, pairs * TILE * TILE),
        name="attend",
    )(bias, taken, left, right)


def tile_bias(near_mask, motion_count, tiles):
    first = lax.axis_index("seq") * tiles
    total = near_mask.shape[0]
    near = lax.dynamic_slice_in_dim(jnp.pad(near_mask, ((REACH, REACH), (0, 0))), first, tiles + 2 * REACH, 0) == 1
    far = lax.dynamic_slice_in_dim(jnp.pad(motion_count, (REACH, REACH)), first, tiles + 2 * REACH, 0) >= 2
    own = jnp.ones_like(far)
    allowed = jnp.stack([far, near[:, 0], own, near[:, 1], far], axis=1)
    index = first - REACH + jnp.arange(tiles + 2 * REACH)
    others = index[:, None] + jnp.arange(-REACH, REACH + 1)[None, :]
    allowed &= (others >= 0) & (others < total)
    return jnp.where(allowed, 0.0, -1e30).astype(jnp.float32).reshape(-1)


def per_device(query_states, key_states, value_states, output_grad, near_mask, motion_count):
    peers, groups = lax.axis_size("blk"), lax.axis_size("seq")
    up = [(i, i + 1) for i in range(groups - 1)]
    down = [(j, i) for i, j in up]
    arrays = (query_states, key_states, value_states, output_grad)
    bias = tile_bias(near_mask, motion_count, peers)

    taken, results = [], None
    for c in range(CHUNKS):
        packed = pack(arrays, c, peers, (bias,) if c else ())
        taken.append(lax.all_to_all(packed, "blk", split_axis=0, concat_axis=0, tiled=True))
    for c in range(CHUNKS):
        low, high = rims(taken[c])
        left = lax.ppermute(high, "seq", up)
        right = lax.ppermute(low, "seq", down)
        out = attend(bias, taken[c], left, right)
        back = lax.all_to_all(out, "blk", split_axis=0, concat_axis=0, tiled=True)
        results = unpack(back, c, query_states.shape[1], results)
    return tuple(results)


def solution(mesh):
    spec = P(("seq", "blk"), None)
    return jax.shard_map(
        per_device, mesh=mesh, in_specs=(spec,) * 4 + (P(), P()), out_specs=(spec,) * 3, check_vma=False
    )
```

```python
import jax
import jax.numpy as jnp
from jax import lax
from jax.experimental import pallas as pl
from jax.experimental.pallas import tpu as pltpu
from jax.sharding import PartitionSpec as P


HEAD_DIM = 64
TILE = 128
REACH = 2
LANES = 128
WINDOW = 2 * REACH + 1
SCALE = float(HEAD_DIM) ** (-0.5)
AXES = ("seq", "blk")
NT = (((1,), (1,)), ((), ()))
TN = (((0,), (0,)), ((), ()))


def cost(flops, moved, exps=0):
    return pl.CostEstimate(flops=flops, bytes_accessed=moved, transcendentals=exps)


def vmem(count):
    return [pl.BlockSpec(memory_space=pltpu.VMEM)] * count


def pair_up(first, second, start, width):
    rows = first.shape[0]
    parts = 4

    def body(first_ref, second_ref, out_ref, held, in_sem, out_sem):
        step = width // parts
        reads, writes = [], []
        for n, ref in ((0, first_ref), (1, second_ref)):
            for c in range(parts):
                here = held.at[n, :, pl.ds(c * step, step)]
                reads.append(pltpu.make_async_copy(ref.at[:, pl.ds(start + c * step, step)], here, in_sem.at[n, c]))
                writes.append(pltpu.make_async_copy(here, out_ref.at[n, :, pl.ds(c * step, step)], out_sem.at[n, c]))
        for read in reads:
            read.start()
        for read, write in zip(reads, writes):
            read.wait()
            write.start()
        for write in writes:
            write.wait()

    shape = (2, rows, width)
    return pl.pallas_call(
        body,
        in_specs=[pl.BlockSpec(memory_space=pl.ANY)] * 2,
        out_specs=pl.BlockSpec(memory_space=pl.ANY),
        out_shape=jax.ShapeDtypeStruct(shape, jnp.bfloat16),
        scratch_shapes=[
            pltpu.VMEM(shape, jnp.bfloat16),
            pltpu.SemaphoreType.DMA((2, parts)),
            pltpu.SemaphoreType.DMA((2, parts)),
        ],
        cost_estimate=cost(0, 4 * rows * width * 2),
        name="pair_up",
    )(first, second)


def both_heads(block):
    first = lax.broadcasted_iota(jnp.int32, block.shape, 1) < HEAD_DIM
    zero = jnp.zeros_like(block)
    return jnp.concatenate([jnp.where(first, block, zero), jnp.where(first, zero, block)], axis=0)


def over_pairs(count, step):
    def steps(n, _):
        step(2 * n)
        step(2 * n + 1)
        return 0

    lax.fori_loop(0, count // 2, steps, 0)


def query_body(bias_ref, q_ref, g_ref, *refs):
    around, (dquery_ref, stats_ref, acc_ref) = refs[:WINDOW], refs[WINDOW:]

    def step(p):
        cols = pl.ds(pl.multiple_of(p * LANES, LANES), LANES)
        query = both_heads(q_ref[:, cols] * jnp.bfloat16(SCALE))
        grad = both_heads(g_ref[:, cols])
        key = jnp.concatenate([ref[0, :, cols] for ref in around], axis=0)
        value = jnp.concatenate([ref[1, :, cols] for ref in around], axis=0)
        scores = lax.dot_general(key, query, NT, preferred_element_type=jnp.float32)
        scores = jnp.concatenate(
            [scores[t * TILE:(t + 1) * TILE] + bias_ref[t] for t in range(WINDOW)], axis=0)
        top = jnp.max(scores, axis=0, keepdims=True)
        weights = jnp.exp(scores - top)
        inverse = 1.0 / jnp.sum(weights, axis=0, keepdims=True)
        probs = weights * inverse
        probs_b = probs.astype(jnp.bfloat16)
        dprobs = lax.dot_general(value, grad, NT, preferred_element_type=jnp.float32)
        delta = jnp.sum(probs_b.astype(jnp.float32) * dprobs, axis=0, keepdims=True)
        dscores = (probs * (dprobs - delta)).astype(jnp.bfloat16)
        stats_ref[0, pl.ds(p, 1)] = top
        stats_ref[1, pl.ds(p, 1)] = inverse
        stats_ref[2, pl.ds(p, 1)] = delta
        own = slice(REACH * TILE, (REACH + 1) * TILE)
        acc_ref[0, :, cols] = jnp.dot(dscores[own], query, preferred_element_type=jnp.float32)
        acc_ref[1, :, cols] = jnp.dot(probs_b[own], grad, preferred_element_type=jnp.float32)
        dquery = lax.dot_general(dscores, key, TN, preferred_element_type=jnp.float32)
        first = lax.broadcasted_iota(jnp.int32, (TILE, LANES), 1) < HEAD_DIM
        dquery_ref[:, cols] = (jnp.where(first, dquery[:TILE], dquery[TILE:]) * SCALE).astype(jnp.bfloat16)

    over_pairs(q_ref.shape[1] // LANES, step)


def query_side(bias, queries, grads, around):
    rows, columns = queries.shape
    pairs = columns // LANES
    return pl.pallas_call(
        query_body,
        in_specs=[pl.BlockSpec(memory_space=pltpu.SMEM)] + vmem(2 + WINDOW),
        out_specs=vmem(3),
        out_shape=[
            jax.ShapeDtypeStruct((rows, columns), jnp.bfloat16),
            jax.ShapeDtypeStruct((3, pairs, 2 * rows), jnp.float32),
            jax.ShapeDtypeStruct((2, rows, columns), jnp.float32),
        ],
        compiler_params=pltpu.CompilerParams(vmem_limit_bytes=28 << 20),
        cost_estimate=cost(pairs * WINDOW * 8 * TILE * TILE * LANES, 8 << 20, pairs * WINDOW * 2 * TILE * TILE),
        name="query_side",
    )(bias, queries, grads, *around)


def key_side(bias, keys_values, acc, part, parts, others, so_far=None):
    _, rows, columns = keys_values.shape
    width = columns // parts
    pairs = width // LANES
    count = len(others)
    last = so_far is not None
    given = list(so_far) if last else []

    def body(bias_ref, kv_ref, acc_ref, *refs):
        stats, sent = refs[:count], refs[count:2 * count]
        outs = refs[2 * count + len(given):]

        def step(p):
            full = pl.ds(pl.multiple_of((part * pairs + p) * LANES, LANES), LANES)
            cols = pl.ds(pl.multiple_of(p * LANES, LANES), LANES)
            key, value = kv_ref[0, :, full], kv_ref[1, :, full]
            at = full if acc_ref.shape[2] == columns else cols
            dkey, dvalue = acc_ref[0, :, at], acc_ref[1, :, at]
            row = pl.ds(part * pairs + p, 1)
            for n in range(count):
                query = both_heads(sent[n][0, :, cols] * jnp.bfloat16(SCALE))
                grad = both_heads(sent[n][1, :, cols])
                scores = lax.dot_general(key, query, NT, preferred_element_type=jnp.float32)
                scores = scores + bias_ref[WINDOW + REACH + others[n][0]]
                probs = jnp.exp(scores - stats[n][0, row]) * stats[n][1, row]
                dprobs = lax.dot_general(value, grad, NT, preferred_element_type=jnp.float32)
                dscores = (probs * (dprobs - stats[n][2, row])).astype(jnp.bfloat16)
                dkey += jnp.dot(dscores, query, preferred_element_type=jnp.float32)
                dvalue += jnp.dot(probs.astype(jnp.bfloat16), grad, preferred_element_type=jnp.float32)
            if last:
                outs[0][:, cols] = dkey.astype(jnp.bfloat16)
                outs[1][:, cols] = dvalue.astype(jnp.bfloat16)
            else:
                outs[0][0, :, cols] = dkey
                outs[0][1, :, cols] = dvalue

        over_pairs(pairs, step)

    if last:
        out_specs = [pl.BlockSpec((rows, width), lambda _: (0, part))] * 2
        out_shape = [jax.ShapeDtypeStruct((rows, columns), jnp.bfloat16)] * 2
    else:
        out_specs = [pl.BlockSpec((2, rows, width), lambda _: (0, 0, 0))]
        out_shape = [jax.ShapeDtypeStruct((2, rows, width), jnp.float32)]
    whole = [pl.BlockSpec(memory_space=pltpu.VMEM)]
    return pl.pallas_call(
        body,
        grid=(1,),
        in_specs=[pl.BlockSpec(memory_space=pltpu.SMEM)] + whole * (2 + 2 * count)
        + [pl.BlockSpec(memory_space=pl.ANY)] * len(given),
        out_specs=out_specs,
        out_shape=out_shape,
        input_output_aliases={3 + 2 * count + n: n for n in range(len(given))},
        compiler_params=pltpu.CompilerParams(vmem_limit_bytes=28 << 20),
        cost_estimate=cost(pairs * count * 8 * TILE * TILE * LANES, 4 << 20, pairs * count * 2 * TILE * TILE),
        name="key_side",
    )(bias, keys_values, acc, *[o[1] for o in others], *[o[2] for o in others], *given)


def tile_bias(near_mask, motion_count):
    me = lax.axis_index(AXES)
    near = lax.dynamic_slice_in_dim(jnp.pad(near_mask, ((REACH, REACH), (0, 0))), me, WINDOW, 0) == 1
    far = lax.dynamic_slice_in_dim(jnp.pad(motion_count, (REACH, REACH)), me, WINDOW, 0) >= 2
    other = me + jnp.arange(-REACH, REACH + 1)
    real = (other >= 0) & (other < near_mask.shape[0])
    own = jnp.ones((), bool)
    queries = jnp.stack([far[2], near[2, 0], own, near[2, 1], far[2]]) & real
    keys = jnp.stack([far[0], near[1, 1], own, near[3, 0], far[4]]) & real
    return jnp.where(jnp.concatenate([queries, keys]), 0.0, -1e30).astype(jnp.float32)


def shift(x, distance):
    total = lax.axis_size("seq") * lax.axis_size("blk")
    route = [(i, i + distance) for i in range(total) if 0 <= i + distance < total]
    return lax.ppermute(x, AXES, route)


def from_both(below, above):
    left = shift(below, 1)
    right = shift(above, -1)
    return left, right


def per_device(query_states, key_states, value_states, output_grad, near_mask, motion_count):
    columns = query_states.shape[1]
    half = columns // 2
    bias = tile_bias(near_mask, motion_count)
    kv = pair_up(key_states, value_states, 0, columns)
    kv_left, kv_right = from_both(kv, kv)
    kv_left2, kv_right2 = from_both(kv_left, kv_right)
    near, far = [], []
    for part in range(2):
        qg = pair_up(query_states, output_grad, part * half, half)
        near.append(from_both(qg, qg))
        far.append(from_both(*near[part]))
    dquery, stats, acc = query_side(
        bias, query_states, output_grad, [kv_left2, kv_left, kv, kv_right, kv_right2])
    stats_of = {}
    for d in (1, 2, -1, -2):
        stats_of[d] = shift(stats, -d)
    grads = None
    for part in range(2):
        close = [(-1, stats_of[-1], near[part][0]), (1, stats_of[1], near[part][1])]
        wide = [(-2, stats_of[-2], far[part][0]), (2, stats_of[2], far[part][1])]
        (sums,) = key_side(bias, kv, acc, part, 2, close)
        grads = key_side(bias, kv, sums, part, 2, wide, grads if part else ())
    return dquery, grads[0], grads[1]


def solution(mesh):
    spec = P(AXES, None)
    return jax.shard_map(
        per_device, mesh=mesh, in_specs=(spec,) * 4 + (P(), P()), out_specs=(spec,) * 3, check_vma=False
    )
```

```python
import jax
import jax.numpy as jnp
from jax import lax
from jax.experimental import pallas as pl
from jax.experimental.pallas import tpu as pltpu
from jax.sharding import PartitionSpec as P


HEAD_DIM = 64
TILE = 128
REACH = 2
LANES = 128
WINDOW = 2 * REACH + 1
SPAN = WINDOW * TILE
SCALE = float(HEAD_DIM) ** (-0.5)
AXES = ("seq", "blk")
CORES = 2
VMEM = pl.BlockSpec(memory_space=pltpu.VMEM)
NT = (((1,), (1,)), ((), ()))
TN = (((0,), (0,)), ((), ()))


def cost(flops, moved, exps=0):
    return pl.CostEstimate(flops=flops, bytes_accessed=moved, transcendentals=exps)


def pack(arrays, peers):
    rows, count = arrays[0].shape[0], len(arrays)

    def body(*refs):
        ins, refs = refs[:count], refs[count:]
        out_ref, held, in_sem, out_sem = refs
        reads = [
            [
                pltpu.make_async_copy(ins[n].at[:, pl.ds(b * LANES, LANES)], held.at[b, n], in_sem.at[b, n])
                for n in range(count)
            ]
            for b in range(peers)
        ]
        writes = [pltpu.make_async_copy(held.at[b], out_ref.at[b], out_sem.at[b]) for b in range(peers)]
        for b in range(peers):
            for n in range(count):
                reads[b][n].start()
        for b in range(peers):
            for n in range(count):
                reads[b][n].wait()
            writes[b].start()
        for b in range(peers):
            writes[b].wait()

    shape = (peers, count, rows, LANES)
    return pl.pallas_call(
        body,
        in_specs=[pl.BlockSpec(memory_space=pl.ANY)] * count,
        out_specs=pl.BlockSpec(memory_space=pl.ANY),
        out_shape=jax.ShapeDtypeStruct(shape, jnp.bfloat16),
        scratch_shapes=[
            pltpu.VMEM(shape, jnp.bfloat16),
            pltpu.SemaphoreType.DMA((peers, count)),
            pltpu.SemaphoreType.DMA((peers,)),
        ],
        cost_estimate=cost(0, 2 * peers * count * rows * LANES * 2),
        name="pack",
    )(*arrays)


def unpack(grads):
    peers, count, rows, _ = grads.shape

    def body(in_ref, *refs):
        outs, sem = refs[:count], refs[count]
        copies = [
            pltpu.make_async_copy(in_ref.at[b, n], outs[n].at[:, pl.ds(b * LANES, LANES)], sem.at[b, n])
            for b in range(peers)
            for n in range(count)
        ]
        for copy in copies:
            copy.start()
        for copy in copies:
            copy.wait()

    return pl.pallas_call(
        body,
        in_specs=[pl.BlockSpec(memory_space=pl.ANY)],
        out_specs=[pl.BlockSpec(memory_space=pl.ANY)] * count,
        out_shape=[jax.ShapeDtypeStruct((rows, peers * LANES), jnp.bfloat16)] * count,
        scratch_shapes=[pltpu.SemaphoreType.DMA((peers, count))],
        compiler_params=pltpu.CompilerParams(vmem_limit_bytes=4 << 20),
        cost_estimate=cost(0, 2 * peers * count * rows * LANES * 2),
        name="unpack",
    )(grads)


def rim_body(x_ref, after_ref, low_ref, high_ref):
    tiles = x_ref.shape[0]
    deep = 2 * REACH
    for ref, wide, narrow in ((low_ref, 0, 0), (high_ref, tiles - deep, tiles - REACH)):
        for t in range(deep):
            ref[t] = x_ref[wide + t, 1]
            ref[deep + t] = x_ref[wide + t, 2]
        for t in range(REACH):
            ref[2 * deep + t] = x_ref[narrow + t, 0]
            ref[2 * deep + REACH + t] = x_ref[narrow + t, 3]


def rims(taken, after):
    shape = jax.ShapeDtypeStruct((6 * REACH,) + taken.shape[2:], taken.dtype)
    return pl.pallas_call(
        rim_body,
        in_specs=[VMEM, pl.BlockSpec(memory_space=pl.ANY)],
        out_specs=[VMEM] * 2,
        out_shape=[shape] * 2,
        compiler_params=pltpu.CompilerParams(vmem_limit_bytes=8 << 20),
        cost_estimate=cost(0, 2 << 20),
        name="rims",
    )(taken, after)


def both_heads(block):
    first = lax.broadcasted_iota(jnp.int32, block.shape, 1) < HEAD_DIM
    zero = jnp.zeros_like(block)
    return jnp.concatenate([jnp.where(first, block, zero), jnp.where(first, zero, block)], axis=0)


def window_grads(bias_ref, row, query_tile, grad_tile, key, value):
    query = both_heads(query_tile * jnp.bfloat16(SCALE))
    grad = both_heads(grad_tile)
    scores = lax.dot_general(key, query, NT, preferred_element_type=jnp.float32)
    scores = jnp.concatenate(
        [scores[t * TILE:(t + 1) * TILE] + bias_ref[row * WINDOW + t] for t in range(WINDOW)], axis=0)
    top = jnp.max(scores, axis=0, keepdims=True)
    weights = jnp.exp(scores - top)
    probs = weights * (1.0 / jnp.sum(weights, axis=0, keepdims=True))
    probs_b = probs.astype(jnp.bfloat16)
    dprobs = lax.dot_general(value, grad, NT, preferred_element_type=jnp.float32)
    delta = jnp.sum(probs_b.astype(jnp.float32) * dprobs, axis=0, keepdims=True)
    dscores = (probs * (dprobs - delta)).astype(jnp.bfloat16)
    return query, grad, probs_b, dscores


def query_grad(dscores, key):
    both = lax.dot_general(dscores, key, TN, preferred_element_type=jnp.float32)
    first = lax.broadcasted_iota(jnp.int32, (TILE, LANES), 1) < HEAD_DIM
    return (jnp.where(first, both[:TILE], both[TILE:]) * SCALE).astype(jnp.bfloat16)


def inner_body(bias_ref, x_ref, dquery_ref, mid_ref, edge_ref, key_ref, value_ref, dkey_ref, dvalue_ref):
    tiles = x_ref.shape[0]
    deep = 2 * REACH
    for t in range(tiles):
        key_ref[t * TILE:(t + 1) * TILE] = x_ref[t, 1]
        value_ref[t * TILE:(t + 1) * TILE] = x_ref[t, 2]
    dkey_ref[...] = jnp.zeros_like(dkey_ref)
    dvalue_ref[...] = jnp.zeros_like(dvalue_ref)

    def step(n):
        rows = pl.ds(pl.multiple_of(n * TILE, TILE), SPAN)
        key, value = key_ref[rows], value_ref[rows]
        query, grad, probs_b, dscores = window_grads(
            bias_ref, n + 2 * REACH, x_ref[n + REACH, 0], x_ref[n + REACH, 3], key, value)
        dkey_ref[rows] += jnp.dot(dscores, query, preferred_element_type=jnp.float32)
        dvalue_ref[rows] += jnp.dot(probs_b, grad, preferred_element_type=jnp.float32)
        dquery_ref[n] = query_grad(dscores, key)

    def steps(n, _):
        step(2 * n)
        step(2 * n + 1)
        return 0

    lax.fori_loop(0, (tiles - 2 * REACH) // 2, steps, 0)
    for n, ref in ((0, dkey_ref), (1, dvalue_ref)):
        for t in range(tiles):
            block = ref[t * TILE:(t + 1) * TILE]
            if t < deep:
                edge_ref[n, t * TILE:(t + 1) * TILE] = block
            elif t >= tiles - deep:
                at = (t - tiles + 2 * deep) * TILE
                edge_ref[n, at:at + TILE] = block
            else:
                mid_ref[t - deep, n] = block.astype(jnp.bfloat16)


def inner(bias, taken):
    tiles = taken.shape[0]
    steps = tiles - 2 * REACH
    whole = tiles * TILE
    return pl.pallas_call(
        inner_body,
        in_specs=[pl.BlockSpec(memory_space=pltpu.SMEM), VMEM],
        out_specs=[VMEM] * 3,
        out_shape=[
            jax.ShapeDtypeStruct((steps, TILE, LANES), jnp.bfloat16),
            jax.ShapeDtypeStruct((tiles - 4 * REACH, 2, TILE, LANES), jnp.bfloat16),
            jax.ShapeDtypeStruct((2, 4 * REACH * TILE, LANES), jnp.float32),
        ],
        scratch_shapes=[pltpu.VMEM((whole, LANES), jnp.bfloat16)] * 2 + [pltpu.VMEM((whole, LANES), jnp.float32)] * 2,
        compiler_params=pltpu.CompilerParams(vmem_limit_bytes=28 << 20),
        cost_estimate=cost(steps * WINDOW * 10 * TILE * TILE * LANES, 5 << 20, steps * WINDOW * 2 * TILE * TILE),
        name="inner",
    )(bias, taken)


def outer_body(bias_ref, x_ref, low_ref, high_ref, dquery_ref, mid_ref, edge_ref, out_ref, key_ref, value_ref, acc_ref):
    tiles = x_ref.shape[0]
    deep = 2 * REACH
    for n, ref in ((1, key_ref), (2, value_ref)):
        for t in range(deep):
            ref[t * TILE:(t + 1) * TILE] = low_ref[(n - 1) * deep + t]
            ref[(deep + t) * TILE:(deep + t + 1) * TILE] = x_ref[t, n]
            ref[(2 * deep + t) * TILE:(2 * deep + t + 1) * TILE] = x_ref[tiles - deep + t, n]
            ref[(3 * deep + t) * TILE:(3 * deep + t + 1) * TILE] = high_ref[(n - 1) * deep + t]
    acc_ref[...] = edge_ref[...]
    for t in range(tiles - 2 * REACH):
        out_ref[REACH + t, 0] = dquery_ref[t]
    for t in range(tiles - 2 * deep):
        out_ref[deep + t, 1] = mid_ref[t, 0]
        out_ref[deep + t, 2] = mid_ref[t, 1]
    for j in range(deep):
        for high in (False, True):
            start = j + (2 * deep if high else 0)
            rows = slice(start * TILE, (start + WINDOW) * TILE)
            key, value = key_ref[rows], value_ref[rows]
            own = (j < REACH) == high
            tile = (tiles - REACH + j if high else j - REACH) if own else None
            row = j + tiles if high else j
            if own:
                query_tile, grad_tile = x_ref[tile, 0], x_ref[tile, 3]
            else:
                ref, at = (high_ref, j - REACH) if high else (low_ref, j)
                query_tile, grad_tile = ref[2 * deep + at], ref[2 * deep + REACH + at]
            query, grad, probs_b, dscores = window_grads(bias_ref, row, query_tile, grad_tile, key, value)
            if high:
                first, last = max(start, 2 * deep), min(start + WINDOW, 3 * deep)
            else:
                first, last = max(start, deep), min(start + WINDOW, 2 * deep)
            part = slice((first - start) * TILE, (last - start) * TILE)
            at = slice((first - deep) * TILE, (last - deep) * TILE)
            acc_ref[0, at] += jnp.dot(dscores[part], query, preferred_element_type=jnp.float32)
            acc_ref[1, at] += jnp.dot(probs_b[part], grad, preferred_element_type=jnp.float32)
            if own:
                out_ref[tile, 0] = query_grad(dscores, key)
    for n in range(2):
        for t in range(2 * deep):
            tile = t if t < deep else tiles - 2 * deep + t
            out_ref[tile, 1 + n] = acc_ref[n, t * TILE:(t + 1) * TILE].astype(jnp.bfloat16)


def outer(bias, taken, low, high, dquery, mid, edge):
    tiles = taken.shape[0]
    steps = 4 * REACH
    return pl.pallas_call(
        outer_body,
        in_specs=[pl.BlockSpec(memory_space=pltpu.SMEM)] + [VMEM] * 6,
        out_specs=VMEM,
        out_shape=jax.ShapeDtypeStruct((tiles, 3, TILE, LANES), jnp.bfloat16),
        scratch_shapes=[pltpu.VMEM((8 * REACH * TILE, LANES), jnp.bfloat16)] * 2
        + [pltpu.VMEM(edge.shape, jnp.float32)],
        compiler_params=pltpu.CompilerParams(vmem_limit_bytes=28 << 20),
        cost_estimate=cost(steps * WINDOW * 8 * TILE * TILE * LANES, 6 << 20, steps * WINDOW * 2 * TILE * TILE),
        name="outer",
    )(bias, taken, low, high, dquery, mid, edge)


def tile_bias(near_mask, motion_count, first, tiles):
    total = near_mask.shape[0]
    near = lax.dynamic_slice_in_dim(jnp.pad(near_mask, ((REACH, REACH), (0, 0))), first, tiles + 2 * REACH, 0) == 1
    far = lax.dynamic_slice_in_dim(jnp.pad(motion_count, (REACH, REACH)), first, tiles + 2 * REACH, 0) >= 2
    own = jnp.ones_like(far)
    allowed = jnp.stack([far, near[:, 0], own, near[:, 1], far], axis=1)
    index = first - REACH + jnp.arange(tiles + 2 * REACH)
    others = index[:, None] + jnp.arange(-REACH, REACH + 1)[None, :]
    allowed &= (others >= 0) & (others < total)
    return jnp.where(allowed, 0.0, -1e30).astype(jnp.float32).reshape(-1)


def per_device(query_states, key_states, value_states, output_grad, near_mask, motion_count):
    blocks, spans = lax.axis_size("blk"), lax.axis_size("seq")
    tiles = CORES * blocks
    groups = [[g * tiles + t for t in range(tiles)] for g in range(spans // CORES)]

    def exchange(x):
        return lax.all_to_all(x, AXES, split_axis=0, concat_axis=0, tiled=True, axis_index_groups=groups)

    up = [(i, i + CORES) for i in range(spans - CORES)]
    down = [(j, i) for i, j in up]
    bias = tile_bias(near_mask, motion_count, lax.axis_index("seq") // CORES * tiles, tiles)
    packed = pack((query_states, key_states, value_states, output_grad), tiles)
    taken = exchange(packed)
    first, last = rims(taken, bias)
    low = lax.ppermute(last, "seq", up)
    high = lax.ppermute(first, "seq", down)
    parts = inner(bias, taken)
    out = outer(bias, taken, low, high, *parts)
    back = exchange(out)
    return tuple(unpack(back))


def solution(mesh):
    spec = P(AXES, None)
    return jax.shard_map(
        per_device, mesh=mesh, in_specs=(spec,) * 4 + (P(), P()), out_specs=(spec,) * 3, check_vma=False
    )
```

```python
import jax
import jax.numpy as jnp
from jax import lax
from jax.experimental import pallas as pl
from jax.experimental.pallas import tpu as pltpu
from jax.sharding import PartitionSpec as P


HEAD_DIM = 64
TILE = 128
REACH = 2
LANES = 128
WINDOW = 2 * REACH + 1
SPAN = WINDOW * TILE
SCALE = float(HEAD_DIM) ** (-0.5)
AXES = ("seq", "blk")
CORES = 2
VMEM = pl.BlockSpec(memory_space=pltpu.VMEM)
NT = (((1,), (1,)), ((), ()))
TN = (((0,), (0,)), ((), ()))


def cost(flops, moved, exps=0):
    return pl.CostEstimate(flops=flops, bytes_accessed=moved, transcendentals=exps)


def pack(arrays, peers):
    rows, count = arrays[0].shape[0], len(arrays)

    def body(*refs):
        ins, refs = refs[:count], refs[count:]
        out_ref, held, in_sem, out_sem = refs
        reads = [
            [
                pltpu.make_async_copy(ins[n].at[:, pl.ds(b * LANES, LANES)], held.at[b, n], in_sem.at[b, n])
                for n in range(count)
            ]
            for b in range(peers)
        ]
        writes = [pltpu.make_async_copy(held.at[b], out_ref.at[b], out_sem.at[b]) for b in range(peers)]
        for b in range(peers):
            for n in range(count):
                reads[b][n].start()
        for b in range(peers):
            for n in range(count):
                reads[b][n].wait()
            writes[b].start()
        for b in range(peers):
            writes[b].wait()

    shape = (peers, count, rows, LANES)
    return pl.pallas_call(
        body,
        in_specs=[pl.BlockSpec(memory_space=pl.ANY)] * count,
        out_specs=pl.BlockSpec(memory_space=pl.ANY),
        out_shape=jax.ShapeDtypeStruct(shape, jnp.bfloat16),
        scratch_shapes=[
            pltpu.VMEM(shape, jnp.bfloat16),
            pltpu.SemaphoreType.DMA((peers, count)),
            pltpu.SemaphoreType.DMA((peers,)),
        ],
        cost_estimate=cost(0, 2 * peers * count * rows * LANES * 2),
        name="pack",
    )(*arrays)


def unpack(grads):
    peers, count, rows, _ = grads.shape

    def body(in_ref, *refs):
        outs, sem = refs[:count], refs[count]
        copies = [
            pltpu.make_async_copy(in_ref.at[b, n], outs[n].at[:, pl.ds(b * LANES, LANES)], sem.at[b, n])
            for b in range(peers)
            for n in range(count)
        ]
        for copy in copies:
            copy.start()
        for copy in copies:
            copy.wait()

    return pl.pallas_call(
        body,
        in_specs=[pl.BlockSpec(memory_space=pl.ANY)],
        out_specs=[pl.BlockSpec(memory_space=pl.ANY)] * count,
        out_shape=[jax.ShapeDtypeStruct((rows, peers * LANES), jnp.bfloat16)] * count,
        scratch_shapes=[pltpu.SemaphoreType.DMA((peers, count))],
        compiler_params=pltpu.CompilerParams(vmem_limit_bytes=4 << 20),
        cost_estimate=cost(0, 2 * peers * count * rows * LANES * 2),
        name="unpack",
    )(grads)


def rim_body(info_ref, x_ref, first_ref, second_ref):
    tiles = x_ref.shape[0]
    deep = 2 * REACH
    odd = info_ref[info_ref.shape[0] - 1] > 0.5
    for ref, low in ((first_ref, odd), (second_ref, jnp.logical_not(odd))):
        wide = jnp.where(low, 0, tiles - deep)
        narrow = jnp.where(low, 0, tiles - REACH)
        for t in range(deep):
            ref[t] = x_ref[wide + t, 1]
            ref[deep + t] = x_ref[wide + t, 2]
        for t in range(REACH):
            ref[2 * deep + t] = x_ref[narrow + t, 0]
            ref[2 * deep + REACH + t] = x_ref[narrow + t, 3]


def rims(info, taken):
    shape = jax.ShapeDtypeStruct((6 * REACH,) + taken.shape[2:], taken.dtype)
    return pl.pallas_call(
        rim_body,
        in_specs=[pl.BlockSpec(memory_space=pltpu.SMEM), VMEM],
        out_specs=[VMEM] * 2,
        out_shape=[shape] * 2,
        compiler_params=pltpu.CompilerParams(vmem_limit_bytes=8 << 20),
        cost_estimate=cost(0, 2 << 20),
        name="rims",
    )(info, taken)


def both_heads(block):
    first = lax.broadcasted_iota(jnp.int32, block.shape, 1) < HEAD_DIM
    zero = jnp.zeros_like(block)
    return jnp.concatenate([jnp.where(first, block, zero), jnp.where(first, zero, block)], axis=0)


def score_stage(bias_ref, row, query_tile, grad_tile, key, value, held):
    scores_ref, dprobs_ref, query_ref, grad_ref = held[:4]
    query = both_heads(query_tile * jnp.bfloat16(SCALE))
    grad = both_heads(grad_tile)
    scores = lax.dot_general(key, query, NT, preferred_element_type=jnp.float32)
    for t in range(WINDOW):
        rows = slice(t * TILE, (t + 1) * TILE)
        scores_ref[rows] = scores[rows] + bias_ref[row * WINDOW + t]
    dprobs_ref[...] = lax.dot_general(value, grad, NT, preferred_element_type=jnp.float32)
    query_ref[...] = query
    grad_ref[...] = grad


def softmax_stage(held):
    scores_ref, dprobs_ref, _, _, probs_ref, dscores_ref = held
    parts = [slice(t * TILE, (t + 1) * TILE) for t in range(WINDOW)]
    top = jnp.max(scores_ref[...], axis=0, keepdims=True)
    total = jnp.zeros_like(top)
    for rows in parts:
        weights = jnp.exp(scores_ref[rows] - top)
        scores_ref[rows] = weights
        total += jnp.sum(weights, axis=0, keepdims=True)
    inverse = 1.0 / total
    delta = jnp.zeros_like(top)
    for rows in parts:
        probs = (scores_ref[rows] * inverse).astype(jnp.bfloat16)
        probs_ref[rows] = probs
        delta += jnp.sum(probs.astype(jnp.float32) * dprobs_ref[rows], axis=0, keepdims=True)
    for rows in parts:
        dscores_ref[rows] = (scores_ref[rows] * inverse * (dprobs_ref[rows] - delta)).astype(jnp.bfloat16)


def held_shapes():
    wide, tall = (SPAN, 2 * TILE), (2 * TILE, LANES)
    return [pltpu.VMEM(wide, jnp.float32)] * 2 + [pltpu.VMEM(tall, jnp.bfloat16)] * 2 + [pltpu.VMEM(wide, jnp.bfloat16)] * 2


def query_grad(dscores, key):
    both = lax.dot_general(dscores, key, TN, preferred_element_type=jnp.float32)
    first = lax.broadcasted_iota(jnp.int32, (TILE, LANES), 1) < HEAD_DIM
    return (jnp.where(first, both[:TILE], both[TILE:]) * SCALE).astype(jnp.bfloat16)


def inner_body(bias_ref, x_ref, dquery_ref, mid_ref, edge_ref, key_ref, value_ref, dkey_ref, dvalue_ref, *held):
    tiles = x_ref.shape[0]
    deep = 2 * REACH
    held = (held[:6], held[6:])
    for t in range(tiles):
        key_ref[t * TILE:(t + 1) * TILE] = x_ref[t, 1]
        value_ref[t * TILE:(t + 1) * TILE] = x_ref[t, 2]
    dkey_ref[...] = jnp.zeros_like(dkey_ref)
    dvalue_ref[...] = jnp.zeros_like(dvalue_ref)

    def rows_of(n):
        return pl.ds(n * TILE if isinstance(n, int) else pl.multiple_of(n * TILE, TILE), SPAN)

    def begin(n, slot):
        rows = rows_of(n)
        score_stage(
            bias_ref, n + 2 * REACH, x_ref[n + REACH, 0], x_ref[n + REACH, 3], key_ref[rows], value_ref[rows], held[slot])

    def end(n, slot):
        _, _, query_ref, grad_ref, probs_ref, dscores_ref = held[slot]
        rows = rows_of(n)
        dscores = dscores_ref[...]
        dkey_ref[rows] += jnp.dot(dscores, query_ref[...], preferred_element_type=jnp.float32)
        dvalue_ref[rows] += jnp.dot(probs_ref[...], grad_ref[...], preferred_element_type=jnp.float32)
        dquery_ref[n] = query_grad(dscores, key_ref[rows])

    steps = tiles - 2 * REACH
    begin(0, 0)
    softmax_stage(held[0])
    begin(1, 1)

    def pair(k, _):
        n = 2 * k
        end(n, 0)
        softmax_stage(held[1])
        begin(n + 2, 0)
        end(n + 1, 1)
        softmax_stage(held[0])
        begin(n + 3, 1)
        return 0

    lax.fori_loop(0, steps // 2 - 1, pair, 0)
    end(steps - 2, 0)
    softmax_stage(held[1])
    end(steps - 1, 1)
    for n, ref in ((0, dkey_ref), (1, dvalue_ref)):
        for t in range(tiles):
            block = ref[t * TILE:(t + 1) * TILE]
            if t < deep:
                edge_ref[n, t * TILE:(t + 1) * TILE] = block
            elif t >= tiles - deep:
                at = (t - tiles + 2 * deep) * TILE
                edge_ref[n, at:at + TILE] = block
            else:
                mid_ref[t - deep, n] = block.astype(jnp.bfloat16)


def inner(bias, taken):
    tiles = taken.shape[0]
    steps = tiles - 2 * REACH
    whole = tiles * TILE
    return pl.pallas_call(
        inner_body,
        in_specs=[pl.BlockSpec(memory_space=pltpu.SMEM), VMEM],
        out_specs=[VMEM] * 3,
        out_shape=[
            jax.ShapeDtypeStruct((steps, TILE, LANES), jnp.bfloat16),
            jax.ShapeDtypeStruct((tiles - 4 * REACH, 2, TILE, LANES), jnp.bfloat16),
            jax.ShapeDtypeStruct((2, 4 * REACH * TILE, LANES), jnp.float32),
        ],
        scratch_shapes=[pltpu.VMEM((whole, LANES), jnp.bfloat16)] * 2 + [pltpu.VMEM((whole, LANES), jnp.float32)] * 2
        + held_shapes() * 2,
        compiler_params=pltpu.CompilerParams(vmem_limit_bytes=28 << 20),
        cost_estimate=cost(steps * WINDOW * 10 * TILE * TILE * LANES, 5 << 20, steps * WINDOW * 2 * TILE * TILE),
        name="inner",
    )(bias, taken)


def outer_body(
    bias_ref, x_ref, first_ref, second_ref, dquery_ref, mid_ref, edge_ref, out_ref, halo_ref, key_ref, value_ref, acc_ref, *held
):
    tiles = x_ref.shape[0]
    deep = 2 * REACH
    held = (held[:6], held[6:])
    odd = bias_ref[bias_ref.shape[0] - 1] > 0.5
    halo_ref[jnp.where(odd, 0, 1)] = first_ref[...]
    halo_ref[jnp.where(odd, 1, 0)] = second_ref[...]
    low_ref, high_ref = halo_ref.at[0], halo_ref.at[1]
    for n, ref in ((1, key_ref), (2, value_ref)):
        for t in range(deep):
            ref[t * TILE:(t + 1) * TILE] = low_ref[(n - 1) * deep + t]
            ref[(deep + t) * TILE:(deep + t + 1) * TILE] = x_ref[t, n]
            ref[(2 * deep + t) * TILE:(2 * deep + t + 1) * TILE] = x_ref[tiles - deep + t, n]
            ref[(3 * deep + t) * TILE:(3 * deep + t + 1) * TILE] = high_ref[(n - 1) * deep + t]
    acc_ref[...] = edge_ref[...]
    for t in range(tiles - 2 * REACH):
        out_ref[REACH + t, 0] = dquery_ref[t]
    for t in range(tiles - 2 * deep):
        out_ref[deep + t, 1] = mid_ref[t, 0]
        out_ref[deep + t, 2] = mid_ref[t, 1]

    def place(step):
        j, high = step // 2, step % 2 == 1
        start = j + (2 * deep if high else 0)
        own = (j < REACH) == high
        tile = (tiles - REACH + j if high else j - REACH) if own else None
        return j, high, start, tile

    def begin(step):
        j, high, start, tile = place(step)
        rows = slice(start * TILE, (start + WINDOW) * TILE)
        if tile is not None:
            query_tile, grad_tile = x_ref[tile, 0], x_ref[tile, 3]
        else:
            ref, at = (high_ref, j - REACH) if high else (low_ref, j)
            query_tile, grad_tile = ref[2 * deep + at], ref[2 * deep + REACH + at]
        score_stage(
            bias_ref, j + tiles if high else j, query_tile, grad_tile, key_ref[rows], value_ref[rows], held[step % 2])

    def end(step):
        _, high, start, tile = place(step)
        _, _, query_ref, grad_ref, probs_ref, dscores_ref = held[step % 2]
        low_end, high_end = (2 * deep, 3 * deep) if high else (deep, 2 * deep)
        first, last = max(start, low_end), min(start + WINDOW, high_end)
        part = slice((first - start) * TILE, (last - start) * TILE)
        at = slice((first - deep) * TILE, (last - deep) * TILE)
        acc_ref[0, at] += jnp.dot(dscores_ref[part], query_ref[...], preferred_element_type=jnp.float32)
        acc_ref[1, at] += jnp.dot(probs_ref[part], grad_ref[...], preferred_element_type=jnp.float32)
        if tile is not None:
            out_ref[tile, 0] = query_grad(dscores_ref[...], key_ref[start * TILE:(start + WINDOW) * TILE])

    steps = 2 * deep
    for step in range(steps + 2):
        if step >= 2:
            end(step - 2)
        if 1 <= step <= steps:
            softmax_stage(held[(step - 1) % 2])
        if step < steps:
            begin(step)
    for n in range(2):
        for t in range(2 * deep):
            tile = t if t < deep else tiles - 2 * deep + t
            out_ref[tile, 1 + n] = acc_ref[n, t * TILE:(t + 1) * TILE].astype(jnp.bfloat16)


def outer(bias, taken, first, second, dquery, mid, edge):
    tiles = taken.shape[0]
    steps = 4 * REACH
    return pl.pallas_call(
        outer_body,
        in_specs=[pl.BlockSpec(memory_space=pltpu.SMEM)] + [VMEM] * 6,
        out_specs=VMEM,
        out_shape=jax.ShapeDtypeStruct((tiles, 3, TILE, LANES), jnp.bfloat16),
        scratch_shapes=[pltpu.VMEM((2,) + first.shape, jnp.bfloat16)]
        + [pltpu.VMEM((8 * REACH * TILE, LANES), jnp.bfloat16)] * 2
        + [pltpu.VMEM(edge.shape, jnp.float32)]
        + held_shapes() * 2,
        compiler_params=pltpu.CompilerParams(vmem_limit_bytes=28 << 20),
        cost_estimate=cost(steps * WINDOW * 8 * TILE * TILE * LANES, 6 << 20, steps * WINDOW * 2 * TILE * TILE),
        name="outer",
    )(bias, taken, first, second, dquery, mid, edge)


def tile_bias(near_mask, motion_count, first, tiles):
    total = near_mask.shape[0]
    near = lax.dynamic_slice_in_dim(jnp.pad(near_mask, ((REACH, REACH), (0, 0))), first, tiles + 2 * REACH, 0) == 1
    far = lax.dynamic_slice_in_dim(jnp.pad(motion_count, (REACH, REACH)), first, tiles + 2 * REACH, 0) >= 2
    own = jnp.ones_like(far)
    allowed = jnp.stack([far, near[:, 0], own, near[:, 1], far], axis=1)
    index = first - REACH + jnp.arange(tiles + 2 * REACH)
    others = index[:, None] + jnp.arange(-REACH, REACH + 1)[None, :]
    allowed &= (others >= 0) & (others < total)
    odd = (first // tiles % 2).astype(jnp.float32)
    return jnp.concatenate([jnp.where(allowed, 0.0, -1e30).astype(jnp.float32).reshape(-1), odd[None]])


def per_device(query_states, key_states, value_states, output_grad, near_mask, motion_count):
    blocks, spans = lax.axis_size("blk"), lax.axis_size("seq")
    tiles = CORES * blocks
    groups = [[g * tiles + t for t in range(tiles)] for g in range(spans // CORES)]

    def exchange(x):
        return lax.all_to_all(x, AXES, split_axis=0, concat_axis=0, tiled=True, axis_index_groups=groups)

    def swap(x, parity):
        right = [(i, i + CORES) for i in range(spans - CORES) if i // CORES % 2 == parity]
        return lax.ppermute(x, "seq", right + [(j, i) for i, j in right])

    bias = tile_bias(near_mask, motion_count, lax.axis_index("seq") // CORES * tiles, tiles)
    packed = pack((query_states, key_states, value_states, output_grad), tiles)
    taken = exchange(packed)
    first, second = rims(bias, taken)
    first = swap(first, 0)
    second = swap(second, 1)
    parts = inner(bias, taken)
    out = outer(bias, taken, first, second, *parts)
    back = exchange(out)
    return tuple(unpack(back))


def solution(mesh):
    spec = P(AXES, None)
    return jax.shard_map(
        per_device, mesh=mesh, in_specs=(spec,) * 4 + (P(), P()), out_specs=(spec,) * 3, check_vma=False
    )
```

```python
import jax
import jax.numpy as jnp
from jax import lax
from jax.experimental import pallas as pl
from jax.experimental.pallas import tpu as pltpu
from jax.sharding import PartitionSpec as P


HEAD_DIM = 64
TILE = 128
REACH = 2
LANES = 128
WINDOW = 2 * REACH + 1
SPAN = WINDOW * TILE
SCALE = float(HEAD_DIM) ** (-0.5)
CHUNKS = 2
VMEM = pl.BlockSpec(memory_space=pltpu.VMEM)
NT = (((1,), (1,)), ((), ()))
TN = (((0,), (0,)), ((), ()))


def cost(flops, moved, exps=0):
    return pl.CostEstimate(flops=flops, bytes_accessed=moved, transcendentals=exps)


def pack(arrays, chunk, peers, after=()):
    rows, count = arrays[0].shape[0], len(arrays)

    def body(*refs):
        ins, refs = refs[:count], refs[count + len(after):]
        out_ref, held, in_sem, out_sem = refs
        reads = [
            [
                pltpu.make_async_copy(
                    ins[n].at[:, pl.ds((chunk * peers + b) * LANES, LANES)], held.at[b, n], in_sem.at[b, n])
                for n in range(count)
            ]
            for b in range(peers)
        ]
        writes = [pltpu.make_async_copy(held.at[b], out_ref.at[b], out_sem.at[b]) for b in range(peers)]
        for b in range(peers):
            for n in range(count):
                reads[b][n].start()
        for b in range(peers):
            for n in range(count):
                reads[b][n].wait()
            writes[b].start()
        for b in range(peers):
            writes[b].wait()

    shape = (peers, count, rows, LANES)
    return pl.pallas_call(
        body,
        in_specs=[pl.BlockSpec(memory_space=pl.ANY)] * (count + len(after)),
        out_specs=pl.BlockSpec(memory_space=pl.ANY),
        out_shape=jax.ShapeDtypeStruct(shape, jnp.bfloat16),
        scratch_shapes=[
            pltpu.VMEM(shape, jnp.bfloat16),
            pltpu.SemaphoreType.DMA((peers, count)),
            pltpu.SemaphoreType.DMA((peers,)),
        ],
        cost_estimate=cost(0, 2 * peers * count * rows * LANES * 2),
        name="pack",
    )(*arrays, *after)


def unpack(grads, chunk, columns, so_far=None):
    peers, count, rows, _ = grads.shape
    given = [] if so_far is None else list(so_far)

    def body(in_ref, *refs):
        outs, sem = refs[len(given):len(given) + count], refs[len(given) + count]
        copies = [
            pltpu.make_async_copy(
                in_ref.at[b, n], outs[n].at[:, pl.ds((chunk * peers + b) * LANES, LANES)], sem.at[b, n])
            for b in range(peers)
            for n in range(count)
        ]
        for copy in copies:
            copy.start()
        for copy in copies:
            copy.wait()

    hbm = pl.BlockSpec(memory_space=pl.ANY)
    return pl.pallas_call(
        body,
        in_specs=[hbm] * (1 + len(given)),
        out_specs=[hbm] * count,
        out_shape=[jax.ShapeDtypeStruct((rows, columns), jnp.bfloat16)] * count,
        scratch_shapes=[pltpu.SemaphoreType.DMA((peers, count))],
        input_output_aliases={1 + n: n for n in range(len(given))},
        compiler_params=pltpu.CompilerParams(vmem_limit_bytes=4 << 20),
        cost_estimate=cost(0, 2 * peers * count * rows * LANES * 2),
        name="unpack",
    )(grads, *given)


def rim_body(info_ref, x_ref, first_ref, second_ref):
    tiles = x_ref.shape[0]
    deep = 2 * REACH
    odd = info_ref[info_ref.shape[0] - 1] > 0.5
    for ref, low in ((first_ref, odd), (second_ref, jnp.logical_not(odd))):
        wide = jnp.where(low, 0, tiles - deep)
        narrow = jnp.where(low, 0, tiles - REACH)
        for t in range(deep):
            ref[t] = x_ref[wide + t, 1]
            ref[deep + t] = x_ref[wide + t, 2]
        for t in range(REACH):
            ref[2 * deep + t] = x_ref[narrow + t, 0]
            ref[2 * deep + REACH + t] = x_ref[narrow + t, 3]


def rims(info, taken):
    shape = jax.ShapeDtypeStruct((6 * REACH,) + taken.shape[2:], taken.dtype)
    return pl.pallas_call(
        rim_body,
        in_specs=[pl.BlockSpec(memory_space=pltpu.SMEM), VMEM],
        out_specs=[VMEM] * 2,
        out_shape=[shape] * 2,
        compiler_params=pltpu.CompilerParams(vmem_limit_bytes=8 << 20),
        cost_estimate=cost(0, 2 << 20),
        name="rims",
    )(info, taken)


def both_heads(block):
    first = lax.broadcasted_iota(jnp.int32, block.shape, 1) < HEAD_DIM
    zero = jnp.zeros_like(block)
    return jnp.concatenate([jnp.where(first, block, zero), jnp.where(first, zero, block)], axis=0)


def score_stage(bias_ref, row, query_tile, grad_tile, key, value, held):
    scores_ref, dprobs_ref, query_ref, grad_ref = held[:4]
    query = both_heads(query_tile * jnp.bfloat16(SCALE))
    grad = both_heads(grad_tile)
    scores = lax.dot_general(key, query, NT, preferred_element_type=jnp.float32)
    for t in range(WINDOW):
        rows = slice(t * TILE, (t + 1) * TILE)
        scores_ref[rows] = scores[rows] + bias_ref[row * WINDOW + t]
    dprobs_ref[...] = lax.dot_general(value, grad, NT, preferred_element_type=jnp.float32)
    query_ref[...] = query
    grad_ref[...] = grad


def softmax_stage(held):
    scores_ref, dprobs_ref, _, _, probs_ref, dscores_ref = held
    parts = [slice(t * TILE, (t + 1) * TILE) for t in range(WINDOW)]
    top = jnp.max(scores_ref[...], axis=0, keepdims=True)
    total = jnp.zeros_like(top)
    for rows in parts:
        weights = jnp.exp(scores_ref[rows] - top)
        scores_ref[rows] = weights
        total += jnp.sum(weights, axis=0, keepdims=True)
    inverse = 1.0 / total
    delta = jnp.zeros_like(top)
    for rows in parts:
        probs = (scores_ref[rows] * inverse).astype(jnp.bfloat16)
        probs_ref[rows] = probs
        delta += jnp.sum(probs.astype(jnp.float32) * dprobs_ref[rows], axis=0, keepdims=True)
    for rows in parts:
        dscores_ref[rows] = (scores_ref[rows] * inverse * (dprobs_ref[rows] - delta)).astype(jnp.bfloat16)


def held_shapes():
    wide, tall = (SPAN, 2 * TILE), (2 * TILE, LANES)
    return [pltpu.VMEM(wide, jnp.float32)] * 2 + [pltpu.VMEM(tall, jnp.bfloat16)] * 2 + [pltpu.VMEM(wide, jnp.bfloat16)] * 2


def query_grad(dscores, key):
    both = lax.dot_general(dscores, key, TN, preferred_element_type=jnp.float32)
    first = lax.broadcasted_iota(jnp.int32, (TILE, LANES), 1) < HEAD_DIM
    return (jnp.where(first, both[:TILE], both[TILE:]) * SCALE).astype(jnp.bfloat16)


def inner_body(bias_ref, x_ref, dquery_ref, edge_ref, key_ref, value_ref, *held):
    tiles = x_ref.shape[0]
    held = (held[:6], held[6:])
    for t in range(tiles):
        key_ref[t * TILE:(t + 1) * TILE] = x_ref[t, 1]
        value_ref[t * TILE:(t + 1) * TILE] = x_ref[t, 2]
    edge_ref[...] = jnp.zeros_like(edge_ref)

    def rows_of(n):
        return pl.ds(n * TILE if isinstance(n, int) else pl.multiple_of(n * TILE, TILE), SPAN)

    def begin(n, slot):
        rows = rows_of(n)
        score_stage(
            bias_ref, n + 2 * REACH, x_ref[n + REACH, 0], x_ref[n + REACH, 3], key_ref[rows], value_ref[rows], held[slot])

    def end(n, slot):
        _, _, query_ref, grad_ref, probs_ref, dscores_ref = held[slot]
        rows = rows_of(n)
        dscores = dscores_ref[...]
        edge_ref[0, rows] += jnp.dot(dscores, query_ref[...], preferred_element_type=jnp.float32)
        edge_ref[1, rows] += jnp.dot(probs_ref[...], grad_ref[...], preferred_element_type=jnp.float32)
        dquery_ref[n] = query_grad(dscores, key_ref[rows])

    steps = tiles - 2 * REACH
    begin(0, 0)
    softmax_stage(held[0])
    begin(1, 1)

    def pair(k, _):
        n = 2 * k
        end(n, 0)
        softmax_stage(held[1])
        begin(n + 2, 0)
        end(n + 1, 1)
        softmax_stage(held[0])
        begin(n + 3, 1)
        return 0

    lax.fori_loop(0, steps // 2 - 1, pair, 0)
    end(steps - 2, 0)
    softmax_stage(held[1])
    end(steps - 1, 1)


def inner(bias, taken):
    tiles = taken.shape[0]
    steps = tiles - 2 * REACH
    whole = tiles * TILE
    return pl.pallas_call(
        inner_body,
        in_specs=[pl.BlockSpec(memory_space=pltpu.SMEM), VMEM],
        out_specs=[VMEM] * 2,
        out_shape=[
            jax.ShapeDtypeStruct((steps, TILE, LANES), jnp.bfloat16),
            jax.ShapeDtypeStruct((2, whole, LANES), jnp.float32),
        ],
        scratch_shapes=[pltpu.VMEM((whole, LANES), jnp.bfloat16)] * 2 + held_shapes() * 2,
        compiler_params=pltpu.CompilerParams(vmem_limit_bytes=28 << 20),
        cost_estimate=cost(steps * WINDOW * 10 * TILE * TILE * LANES, 5 << 20, steps * WINDOW * 2 * TILE * TILE),
        name="inner",
    )(bias, taken)


def outer_body(
    bias_ref, x_ref, first_ref, second_ref, dquery_ref, edge_ref, out_ref, halo_ref, key_ref, value_ref, acc_ref, *held
):
    tiles = x_ref.shape[0]
    deep = 2 * REACH
    held = (held[:6], held[6:])
    odd = bias_ref[bias_ref.shape[0] - 1] > 0.5
    halo_ref[jnp.where(odd, 0, 1)] = first_ref[...]
    halo_ref[jnp.where(odd, 1, 0)] = second_ref[...]
    low_ref, high_ref = halo_ref.at[0], halo_ref.at[1]
    for n, ref in ((1, key_ref), (2, value_ref)):
        for t in range(deep):
            ref[t * TILE:(t + 1) * TILE] = low_ref[(n - 1) * deep + t]
            ref[(deep + t) * TILE:(deep + t + 1) * TILE] = x_ref[t, n]
            ref[(2 * deep + t) * TILE:(2 * deep + t + 1) * TILE] = x_ref[tiles - deep + t, n]
            ref[(3 * deep + t) * TILE:(3 * deep + t + 1) * TILE] = high_ref[(n - 1) * deep + t]
    acc_ref[...] = edge_ref[...]
    for t in range(tiles - 2 * REACH):
        out_ref[REACH + t, 0] = dquery_ref[t]

    def place(step):
        j, high = step // 2, step % 2 == 1
        start = j + (2 * deep if high else 0)
        own = (j < REACH) == high
        tile = (tiles - REACH + j if high else j - REACH) if own else None
        return j, high, start, tile

    def begin(step):
        j, high, start, tile = place(step)
        rows = slice(start * TILE, (start + WINDOW) * TILE)
        if tile is not None:
            query_tile, grad_tile = x_ref[tile, 0], x_ref[tile, 3]
        else:
            ref, at = (high_ref, j - REACH) if high else (low_ref, j)
            query_tile, grad_tile = ref[2 * deep + at], ref[2 * deep + REACH + at]
        score_stage(
            bias_ref, j + tiles if high else j, query_tile, grad_tile, key_ref[rows], value_ref[rows], held[step % 2])

    def end(step):
        _, high, start, tile = place(step)
        _, _, query_ref, grad_ref, probs_ref, dscores_ref = held[step % 2]
        low_end, high_end = (2 * deep, 3 * deep) if high else (deep, 2 * deep)
        first, last = max(start, low_end), min(start + WINDOW, high_end)
        part = slice((first - start) * TILE, (last - start) * TILE)
        at = slice((first - deep) * TILE, (last - deep) * TILE)
        acc_ref[0, at] += jnp.dot(dscores_ref[part], query_ref[...], preferred_element_type=jnp.float32)
        acc_ref[1, at] += jnp.dot(probs_ref[part], grad_ref[...], preferred_element_type=jnp.float32)
        if tile is not None:
            out_ref[tile, 0] = query_grad(dscores_ref[...], key_ref[start * TILE:(start + WINDOW) * TILE])

    steps = 2 * deep
    for step in range(steps + 2):
        if step >= 2:
            end(step - 2)
        if 1 <= step <= steps:
            softmax_stage(held[(step - 1) % 2])
        if step < steps:
            begin(step)
    for n in range(2):
        for t in range(2 * deep):
            tile = t if t < deep else tiles - 2 * deep + t
            out_ref[tile, 1 + n] = acc_ref[n, t * TILE:(t + 1) * TILE].astype(jnp.bfloat16)


def outer(bias, taken, first, second, dquery, edge):
    tiles = taken.shape[0]
    steps = 4 * REACH
    return pl.pallas_call(
        outer_body,
        in_specs=[pl.BlockSpec(memory_space=pltpu.SMEM)] + [VMEM] * 5,
        out_specs=VMEM,
        out_shape=jax.ShapeDtypeStruct((tiles, 3, TILE, LANES), jnp.bfloat16),
        scratch_shapes=[pltpu.VMEM((2,) + first.shape, jnp.bfloat16)]
        + [pltpu.VMEM((8 * REACH * TILE, LANES), jnp.bfloat16)] * 2
        + [pltpu.VMEM(edge.shape, jnp.float32)]
        + held_shapes() * 2,
        compiler_params=pltpu.CompilerParams(vmem_limit_bytes=28 << 20),
        cost_estimate=cost(steps * WINDOW * 8 * TILE * TILE * LANES, 6 << 20, steps * WINDOW * 2 * TILE * TILE),
        name="outer",
    )(bias, taken, first, second, dquery, edge)


def tile_bias(near_mask, motion_count, first, tiles):
    total = near_mask.shape[0]
    near = lax.dynamic_slice_in_dim(jnp.pad(near_mask, ((REACH, REACH), (0, 0))), first, tiles + 2 * REACH, 0) == 1
    far = lax.dynamic_slice_in_dim(jnp.pad(motion_count, (REACH, REACH)), first, tiles + 2 * REACH, 0) >= 2
    own = jnp.ones_like(far)
    allowed = jnp.stack([far, near[:, 0], own, near[:, 1], far], axis=1)
    index = first - REACH + jnp.arange(tiles + 2 * REACH)
    others = index[:, None] + jnp.arange(-REACH, REACH + 1)[None, :]
    allowed &= (others >= 0) & (others < total)
    odd = (first // tiles % 2).astype(jnp.float32)
    return jnp.concatenate([jnp.where(allowed, 0.0, -1e30).astype(jnp.float32).reshape(-1), odd[None]])


def per_device(query_states, key_states, value_states, output_grad, near_mask, motion_count):
    tiles, groups = lax.axis_size("blk"), lax.axis_size("seq")
    columns = query_states.shape[1]
    arrays = (query_states, key_states, value_states, output_grad)

    def exchange(x):
        return lax.all_to_all(x, "blk", split_axis=0, concat_axis=0, tiled=True)

    def swap(x, parity):
        right = [(i, i + 1) for i in range(groups - 1) if i % 2 == parity]
        return lax.ppermute(x, "seq", right + [(j, i) for i, j in right])

    taken, results = [], None
    bias = tile_bias(near_mask, motion_count, lax.axis_index("seq") * tiles, tiles)
    for c in range(CHUNKS):
        packed = pack(arrays, c, tiles, (bias,) if c else ())
        taken.append(exchange(packed))
    for c in range(CHUNKS):
        first, second = rims(bias, taken[c])
        first = swap(first, 0)
        second = swap(second, 1)
        parts = inner(bias, taken[c])
        out = outer(bias, taken[c], first, second, *parts)
        back = exchange(out)
        results = unpack(back, c, columns, results)
    return tuple(results)


def solution(mesh):
    spec = P(("seq", "blk"), None)
    return jax.shard_map(
        per_device, mesh=mesh, in_specs=(spec,) * 4 + (P(), P()), out_specs=(spec,) * 3, check_vma=False
    )
```

```python
import jax
import jax.numpy as jnp
from jax import lax
from jax.experimental import pallas as pl
from jax.experimental.pallas import tpu as pltpu
from jax.sharding import PartitionSpec as P


HEAD_DIM = 64
TILE = 128
REACH = 2
LANES = 128
WINDOW = 2 * REACH + 1
SPAN = WINDOW * TILE
SCALE = float(HEAD_DIM) ** (-0.5)
CHUNKS = 2
ORDER = (4, 3, 5, 2, 6, 1, 7)
VMEM = pl.BlockSpec(memory_space=pltpu.VMEM)
NT = (((1,), (1,)), ((), ()))
TN = (((0,), (0,)), ((), ()))


def cost(flops, moved, exps=0):
    return pl.CostEstimate(flops=flops, bytes_accessed=moved, transcendentals=exps)


def pack(arrays, chunk, peers):
    rows, count = arrays[0].shape[0], len(arrays)

    def body(*refs):
        ins, refs = refs[:count], refs[count:]
        out_ref, held, in_sem, out_sem = refs
        reads = [
            [
                pltpu.make_async_copy(
                    ins[n].at[:, pl.ds((chunk * peers + b) * LANES, LANES)], held.at[b, n], in_sem.at[b, n])
                for n in range(count)
            ]
            for b in range(peers)
        ]
        writes = [pltpu.make_async_copy(held.at[b], out_ref.at[b], out_sem.at[b]) for b in range(peers)]
        for b in range(peers):
            for n in range(count):
                reads[b][n].start()
        for b in range(peers):
            for n in range(count):
                reads[b][n].wait()
            writes[b].start()
        for b in range(peers):
            writes[b].wait()

    shape = (peers, count, rows, LANES)
    return pl.pallas_call(
        body,
        in_specs=[pl.BlockSpec(memory_space=pl.ANY)] * count,
        out_specs=pl.BlockSpec(memory_space=pl.ANY),
        out_shape=jax.ShapeDtypeStruct(shape, jnp.bfloat16),
        scratch_shapes=[
            pltpu.VMEM(shape, jnp.bfloat16),
            pltpu.SemaphoreType.DMA((peers, count)),
            pltpu.SemaphoreType.DMA((peers,)),
        ],
        cost_estimate=cost(0, 2 * peers * count * rows * LANES * 2),
        name="pack",
    )(*arrays)


def pack_around(arrays, chunk, peers, me):
    rows, count = arrays[0].shape[0], len(arrays)

    def body(me_ref, *refs):
        ins, outs = refs[:count], refs[count:count + peers]
        held, in_sem, out_sem = refs[count + peers:]
        reads, writes = [], []
        for b in range(peers):
            at = pl.multiple_of((chunk * peers + (me_ref[0] + b) % peers) * LANES, LANES)
            reads.append([
                pltpu.make_async_copy(ins[n].at[:, pl.ds(at, LANES)], held.at[b, n], in_sem.at[b, n])
                for n in range(count)
            ])
            writes.append(pltpu.make_async_copy(held.at[b], outs[b], out_sem.at[b]))
        for b in range(peers):
            for n in range(count):
                reads[b][n].start()
        for b in range(peers):
            for n in range(count):
                reads[b][n].wait()
            writes[b].start()
        for b in range(peers):
            writes[b].wait()

    block = (count, rows, LANES)
    hbm = pl.BlockSpec(memory_space=pl.ANY)
    return pl.pallas_call(
        body,
        in_specs=[pl.BlockSpec(memory_space=pltpu.SMEM)] + [hbm] * count,
        out_specs=[hbm] * peers,
        out_shape=[jax.ShapeDtypeStruct(block, jnp.bfloat16)] * peers,
        scratch_shapes=[
            pltpu.VMEM((peers,) + block, jnp.bfloat16),
            pltpu.SemaphoreType.DMA((peers, count)),
            pltpu.SemaphoreType.DMA((peers,)),
        ],
        cost_estimate=cost(0, 2 * peers * count * rows * LANES * 2),
        name="pack_around",
    )(me, *arrays)


def join(blocks, me):
    peers = len(blocks)

    def body(me_ref, *refs):
        for n in range(peers):
            refs[peers][(me_ref[0] + peers - n) % peers] = refs[n][...]

    return pl.pallas_call(
        body,
        in_specs=[pl.BlockSpec(memory_space=pltpu.SMEM)] + [VMEM] * peers,
        out_specs=VMEM,
        out_shape=jax.ShapeDtypeStruct((peers,) + blocks[0].shape, blocks[0].dtype),
        compiler_params=pltpu.CompilerParams(vmem_limit_bytes=8 << 20),
        cost_estimate=cost(0, 2 << 20),
        name="join",
    )(me, *blocks)


def unpack(grads, chunk, columns, so_far=None):
    peers, count, rows, _ = grads.shape
    given = [] if so_far is None else list(so_far)

    def body(in_ref, *refs):
        outs, sem = refs[len(given):len(given) + count], refs[len(given) + count]
        copies = [
            pltpu.make_async_copy(
                in_ref.at[b, n], outs[n].at[:, pl.ds((chunk * peers + b) * LANES, LANES)], sem.at[b, n])
            for b in range(peers)
            for n in range(count)
        ]
        for copy in copies:
            copy.start()
        for copy in copies:
            copy.wait()

    hbm = pl.BlockSpec(memory_space=pl.ANY)
    return pl.pallas_call(
        body,
        in_specs=[hbm] * (1 + len(given)),
        out_specs=[hbm] * count,
        out_shape=[jax.ShapeDtypeStruct((rows, columns), jnp.bfloat16)] * count,
        scratch_shapes=[pltpu.SemaphoreType.DMA((peers, count))],
        input_output_aliases={1 + n: n for n in range(len(given))},
        compiler_params=pltpu.CompilerParams(vmem_limit_bytes=4 << 20),
        cost_estimate=cost(0, 2 * peers * count * rows * LANES * 2),
        name="unpack",
    )(grads, *given)


def rim_body(info_ref, x_ref, first_ref, second_ref):
    tiles = x_ref.shape[0]
    deep = 2 * REACH
    odd = info_ref[info_ref.shape[0] - 1] > 0.5
    for ref, low in ((first_ref, odd), (second_ref, jnp.logical_not(odd))):
        wide = jnp.where(low, 0, tiles - deep)
        narrow = jnp.where(low, 0, tiles - REACH)
        for t in range(deep):
            ref[t] = x_ref[wide + t, 1]
            ref[deep + t] = x_ref[wide + t, 2]
        for t in range(REACH):
            ref[2 * deep + t] = x_ref[narrow + t, 0]
            ref[2 * deep + REACH + t] = x_ref[narrow + t, 3]


def rims(info, taken):
    shape = jax.ShapeDtypeStruct((6 * REACH,) + taken.shape[2:], taken.dtype)
    return pl.pallas_call(
        rim_body,
        in_specs=[pl.BlockSpec(memory_space=pltpu.SMEM), VMEM],
        out_specs=[VMEM] * 2,
        out_shape=[shape] * 2,
        compiler_params=pltpu.CompilerParams(vmem_limit_bytes=8 << 20),
        cost_estimate=cost(0, 2 << 20),
        name="rims",
    )(info, taken)


def both_heads(block):
    first = lax.broadcasted_iota(jnp.int32, block.shape, 1) < HEAD_DIM
    zero = jnp.zeros_like(block)
    return jnp.concatenate([jnp.where(first, block, zero), jnp.where(first, zero, block)], axis=0)


def score_stage(bias_ref, row, query_tile, grad_tile, key, value, held):
    scores_ref, dprobs_ref, query_ref, grad_ref = held[:4]
    query = both_heads(query_tile * jnp.bfloat16(SCALE))
    grad = both_heads(grad_tile)
    scores = lax.dot_general(key, query, NT, preferred_element_type=jnp.float32)
    for t in range(WINDOW):
        rows = slice(t * TILE, (t + 1) * TILE)
        scores_ref[rows] = scores[rows] + bias_ref[row * WINDOW + t]
    dprobs_ref[...] = lax.dot_general(value, grad, NT, preferred_element_type=jnp.float32)
    query_ref[...] = query
    grad_ref[...] = grad


def softmax_stage(held):
    scores_ref, dprobs_ref, _, _, probs_ref, dscores_ref = held
    parts = [slice(t * TILE, (t + 1) * TILE) for t in range(WINDOW)]
    top = jnp.max(scores_ref[...], axis=0, keepdims=True)
    total = jnp.zeros_like(top)
    for rows in parts:
        weights = jnp.exp(scores_ref[rows] - top)
        scores_ref[rows] = weights
        total += jnp.sum(weights, axis=0, keepdims=True)
    inverse = 1.0 / total
    delta = jnp.zeros_like(top)
    for rows in parts:
        probs = (scores_ref[rows] * inverse).astype(jnp.bfloat16)
        probs_ref[rows] = probs
        delta += jnp.sum(probs.astype(jnp.float32) * dprobs_ref[rows], axis=0, keepdims=True)
    for rows in parts:
        dscores_ref[rows] = (scores_ref[rows] * inverse * (dprobs_ref[rows] - delta)).astype(jnp.bfloat16)


def held_shapes():
    wide, tall = (SPAN, 2 * TILE), (2 * TILE, LANES)
    return [pltpu.VMEM(wide, jnp.float32)] * 2 + [pltpu.VMEM(tall, jnp.bfloat16)] * 2 + [pltpu.VMEM(wide, jnp.bfloat16)] * 2


def query_grad(dscores, key):
    both = lax.dot_general(dscores, key, TN, preferred_element_type=jnp.float32)
    first = lax.broadcasted_iota(jnp.int32, (TILE, LANES), 1) < HEAD_DIM
    return (jnp.where(first, both[:TILE], both[TILE:]) * SCALE).astype(jnp.bfloat16)


def inner_body(bias_ref, x_ref, dquery_ref, edge_ref, key_ref, value_ref, *held):
    tiles = x_ref.shape[0]
    held = (held[:6], held[6:])
    for t in range(tiles):
        key_ref[t * TILE:(t + 1) * TILE] = x_ref[t, 1]
        value_ref[t * TILE:(t + 1) * TILE] = x_ref[t, 2]
    edge_ref[...] = jnp.zeros_like(edge_ref)

    def rows_of(n):
        return pl.ds(n * TILE if isinstance(n, int) else pl.multiple_of(n * TILE, TILE), SPAN)

    def begin(n, slot):
        rows = rows_of(n)
        score_stage(
            bias_ref, n + 2 * REACH, x_ref[n + REACH, 0], x_ref[n + REACH, 3], key_ref[rows], value_ref[rows], held[slot])

    def end(n, slot):
        _, _, query_ref, grad_ref, probs_ref, dscores_ref = held[slot]
        rows = rows_of(n)
        dscores = dscores_ref[...]
        edge_ref[0, rows] += jnp.dot(dscores, query_ref[...], preferred_element_type=jnp.float32)
        edge_ref[1, rows] += jnp.dot(probs_ref[...], grad_ref[...], preferred_element_type=jnp.float32)
        dquery_ref[n] = query_grad(dscores, key_ref[rows])

    steps = tiles - 2 * REACH
    begin(0, 0)
    softmax_stage(held[0])
    begin(1, 1)

    def pair(k, _):
        n = 2 * k
        end(n, 0)
        softmax_stage(held[1])
        begin(n + 2, 0)
        end(n + 1, 1)
        softmax_stage(held[0])
        begin(n + 3, 1)
        return 0

    lax.fori_loop(0, steps // 2 - 1, pair, 0)
    end(steps - 2, 0)
    softmax_stage(held[1])
    end(steps - 1, 1)


def inner(bias, taken):
    tiles = taken.shape[0]
    steps = tiles - 2 * REACH
    whole = tiles * TILE
    return pl.pallas_call(
        inner_body,
        in_specs=[pl.BlockSpec(memory_space=pltpu.SMEM), VMEM],
        out_specs=[VMEM] * 2,
        out_shape=[
            jax.ShapeDtypeStruct((steps, TILE, LANES), jnp.bfloat16),
            jax.ShapeDtypeStruct((2, whole, LANES), jnp.float32),
        ],
        scratch_shapes=[pltpu.VMEM((whole, LANES), jnp.bfloat16)] * 2 + held_shapes() * 2,
        compiler_params=pltpu.CompilerParams(vmem_limit_bytes=28 << 20),
        cost_estimate=cost(steps * WINDOW * 10 * TILE * TILE * LANES, 5 << 20, steps * WINDOW * 2 * TILE * TILE),
        name="inner",
    )(bias, taken)


def outer_body(
    bias_ref, x_ref, first_ref, second_ref, dquery_ref, edge_ref, out_ref, halo_ref, key_ref, value_ref, acc_ref, *held
):
    tiles = x_ref.shape[0]
    deep = 2 * REACH
    held = (held[:6], held[6:])
    odd = bias_ref[bias_ref.shape[0] - 1] > 0.5
    halo_ref[jnp.where(odd, 0, 1)] = first_ref[...]
    halo_ref[jnp.where(odd, 1, 0)] = second_ref[...]
    low_ref, high_ref = halo_ref.at[0], halo_ref.at[1]
    for n, ref in ((1, key_ref), (2, value_ref)):
        for t in range(deep):
            ref[t * TILE:(t + 1) * TILE] = low_ref[(n - 1) * deep + t]
            ref[(deep + t) * TILE:(deep + t + 1) * TILE] = x_ref[t, n]
            ref[(2 * deep + t) * TILE:(2 * deep + t + 1) * TILE] = x_ref[tiles - deep + t, n]
            ref[(3 * deep + t) * TILE:(3 * deep + t + 1) * TILE] = high_ref[(n - 1) * deep + t]
    acc_ref[...] = edge_ref[...]
    for t in range(tiles - 2 * REACH):
        out_ref[REACH + t, 0] = dquery_ref[t]

    def place(step):
        j, high = step // 2, step % 2 == 1
        start = j + (2 * deep if high else 0)
        own = (j < REACH) == high
        tile = (tiles - REACH + j if high else j - REACH) if own else None
        return j, high, start, tile

    def begin(step):
        j, high, start, tile = place(step)
        rows = slice(start * TILE, (start + WINDOW) * TILE)
        if tile is not None:
            query_tile, grad_tile = x_ref[tile, 0], x_ref[tile, 3]
        else:
            ref, at = (high_ref, j - REACH) if high else (low_ref, j)
            query_tile, grad_tile = ref[2 * deep + at], ref[2 * deep + REACH + at]
        score_stage(
            bias_ref, j + tiles if high else j, query_tile, grad_tile, key_ref[rows], value_ref[rows], held[step % 2])

    def end(step):
        _, high, start, tile = place(step)
        _, _, query_ref, grad_ref, probs_ref, dscores_ref = held[step % 2]
        low_end, high_end = (2 * deep, 3 * deep) if high else (deep, 2 * deep)
        first, last = max(start, low_end), min(start + WINDOW, high_end)
        part = slice((first - start) * TILE, (last - start) * TILE)
        at = slice((first - deep) * TILE, (last - deep) * TILE)
        acc_ref[0, at] += jnp.dot(dscores_ref[part], query_ref[...], preferred_element_type=jnp.float32)
        acc_ref[1, at] += jnp.dot(probs_ref[part], grad_ref[...], preferred_element_type=jnp.float32)
        if tile is not None:
            out_ref[tile, 0] = query_grad(dscores_ref[...], key_ref[start * TILE:(start + WINDOW) * TILE])

    steps = 2 * deep
    for step in range(steps + 2):
        if step >= 2:
            end(step - 2)
        if 1 <= step <= steps:
            softmax_stage(held[(step - 1) % 2])
        if step < steps:
            begin(step)
    for n in range(2):
        for t in range(2 * deep):
            tile = t if t < deep else tiles - 2 * deep + t
            out_ref[tile, 1 + n] = acc_ref[n, t * TILE:(t + 1) * TILE].astype(jnp.bfloat16)


def outer(bias, taken, first, second, dquery, edge):
    tiles = taken.shape[0]
    steps = 4 * REACH
    return pl.pallas_call(
        outer_body,
        in_specs=[pl.BlockSpec(memory_space=pltpu.SMEM)] + [VMEM] * 5,
        out_specs=VMEM,
        out_shape=jax.ShapeDtypeStruct((tiles, 3, TILE, LANES), jnp.bfloat16),
        scratch_shapes=[pltpu.VMEM((2,) + first.shape, jnp.bfloat16)]
        + [pltpu.VMEM((8 * REACH * TILE, LANES), jnp.bfloat16)] * 2
        + [pltpu.VMEM(edge.shape, jnp.float32)]
        + held_shapes() * 2,
        compiler_params=pltpu.CompilerParams(vmem_limit_bytes=28 << 20),
        cost_estimate=cost(steps * WINDOW * 8 * TILE * TILE * LANES, 6 << 20, steps * WINDOW * 2 * TILE * TILE),
        name="outer",
    )(bias, taken, first, second, dquery, edge)


def tile_bias(near_mask, motion_count, first, tiles):
    total = near_mask.shape[0]
    near = lax.dynamic_slice_in_dim(jnp.pad(near_mask, ((REACH, REACH), (0, 0))), first, tiles + 2 * REACH, 0) == 1
    far = lax.dynamic_slice_in_dim(jnp.pad(motion_count, (REACH, REACH)), first, tiles + 2 * REACH, 0) >= 2
    own = jnp.ones_like(far)
    allowed = jnp.stack([far, near[:, 0], own, near[:, 1], far], axis=1)
    index = first - REACH + jnp.arange(tiles + 2 * REACH)
    others = index[:, None] + jnp.arange(-REACH, REACH + 1)[None, :]
    allowed &= (others >= 0) & (others < total)
    odd = (first // tiles % 2).astype(jnp.float32)
    return jnp.concatenate([jnp.where(allowed, 0.0, -1e30).astype(jnp.float32).reshape(-1), odd[None]])


def gate(table):
    def body(in_ref, out_ref):
        out_ref[...] = in_ref[...]

    return pl.pallas_call(
        body,
        in_specs=[VMEM],
        out_specs=VMEM,
        out_shape=jax.ShapeDtypeStruct(table.shape, table.dtype),
        compiler_params=pltpu.CompilerParams(vmem_limit_bytes=1 << 20),
        cost_estimate=cost(0, 1 << 10),
        name="gate",
    )(table)


def per_device(query_states, key_states, value_states, output_grad, near_mask, motion_count):
    tiles, groups = lax.axis_size("blk"), lax.axis_size("seq")
    columns = query_states.shape[1]
    arrays = (query_states, key_states, value_states, output_grad)

    def exchange(x):
        return lax.all_to_all(x, "blk", split_axis=0, concat_axis=0, tiled=True)

    def swap(x, parity):
        right = [(i, i + 1) for i in range(groups - 1) if i % 2 == parity]
        return lax.ppermute(x, "seq", right + [(j, i) for i, j in right])

    taken, results = [], None
    bias = tile_bias(near_mask, motion_count, lax.axis_index("seq") * tiles, tiles)
    me = lax.axis_index("blk").reshape(1)
    packed = pack(arrays, 0, tiles)
    taken.append(exchange(packed))
    blocks = list(pack_around(arrays, 1, tiles, me))
    for n in ORDER:
        blocks[n] = lax.ppermute(blocks[n], "blk", [(i, (i + n) % tiles) for i in range(tiles)])
    taken.append(join(blocks, me))
    info = gate(bias)
    for c in range(CHUNKS):
        first, second = rims(info, taken[c])
        first = swap(first, 0)
        second = swap(second, 1)
        parts = inner(info, taken[c])
        out = outer(info, taken[c], first, second, *parts)
        back = exchange(out)
        results = unpack(back, c, columns, results)
    return tuple(results)


def solution(mesh):
    spec = P(("seq", "blk"), None)
    return jax.shard_map(
        per_device, mesh=mesh, in_specs=(spec,) * 4 + (P(), P()), out_specs=(spec,) * 3, check_vma=False
    )
```

```python
import functools

import jax
import jax.numpy as jnp
from jax import lax
from jax.experimental import pallas as pl
from jax.experimental.pallas import tpu as pltpu
from jax.sharding import PartitionSpec as P


HEAD_DIM = 64
TILE = 128
REACH = 2
LANES = 128
WINDOW = 2 * REACH + 1
SPAN = WINDOW * TILE
SCALE = float(HEAD_DIM) ** (-0.5)
CHUNKS = 2
LAUNCH = 16
ORDER = (4, 3, 5, 2, 6, 1, 7)
VMEM = pl.BlockSpec(memory_space=pltpu.VMEM)
NT = (((1,), (1,)), ((), ()))
TN = (((0,), (0,)), ((), ()))


def cost(flops, moved, exps=0):
    return pl.CostEstimate(flops=flops, bytes_accessed=moved, transcendentals=exps)


def pack(arrays, chunk, peers):
    rows, count = arrays[0].shape[0], len(arrays)

    def body(*refs):
        ins, refs = refs[:count], refs[count:]
        out_ref, held, in_sem, out_sem = refs
        reads = [
            [
                pltpu.make_async_copy(
                    ins[n].at[:, pl.ds((chunk * peers + b) * LANES, LANES)], held.at[b, n], in_sem.at[b, n])
                for n in range(count)
            ]
            for b in range(peers)
        ]
        writes = [pltpu.make_async_copy(held.at[b], out_ref.at[b], out_sem.at[b]) for b in range(peers)]
        for b in range(peers):
            for n in range(count):
                reads[b][n].start()
        for b in range(peers):
            for n in range(count):
                reads[b][n].wait()
            writes[b].start()
        for b in range(peers):
            writes[b].wait()

    shape = (peers, count, rows, LANES)
    return pl.pallas_call(
        body,
        in_specs=[pl.BlockSpec(memory_space=pl.ANY)] * count,
        out_specs=pl.BlockSpec(memory_space=pl.ANY),
        out_shape=jax.ShapeDtypeStruct(shape, jnp.bfloat16),
        scratch_shapes=[
            pltpu.VMEM(shape, jnp.bfloat16),
            pltpu.SemaphoreType.DMA((peers, count)),
            pltpu.SemaphoreType.DMA((peers,)),
        ],
        cost_estimate=cost(0, 2 * peers * count * rows * LANES * 2),
        name="pack",
    )(*arrays)


def pack_around(arrays, chunk, peers, me):
    rows, count = arrays[0].shape[0], len(arrays)

    def body(me_ref, *refs):
        ins, outs = refs[:count], refs[count:count + peers]
        held, in_sem, out_sem = refs[count + peers:]
        reads, writes = [], []
        for b in range(peers):
            at = pl.multiple_of((chunk * peers + (me_ref[0] + b) % peers) * LANES, LANES)
            reads.append([
                pltpu.make_async_copy(ins[n].at[:, pl.ds(at, LANES)], held.at[b, n], in_sem.at[b, n])
                for n in range(count)
            ])
            writes.append(pltpu.make_async_copy(held.at[b], outs[b], out_sem.at[b]))
        for b in range(peers):
            for n in range(count):
                reads[b][n].start()
        for b in range(peers):
            for n in range(count):
                reads[b][n].wait()
            writes[b].start()
        for b in range(peers):
            writes[b].wait()

    block = (count, rows, LANES)
    hbm = pl.BlockSpec(memory_space=pl.ANY)
    return pl.pallas_call(
        body,
        in_specs=[pl.BlockSpec(memory_space=pltpu.SMEM)] + [hbm] * count,
        out_specs=[hbm] * peers,
        out_shape=[jax.ShapeDtypeStruct(block, jnp.bfloat16)] * peers,
        scratch_shapes=[
            pltpu.VMEM((peers,) + block, jnp.bfloat16),
            pltpu.SemaphoreType.DMA((peers, count)),
            pltpu.SemaphoreType.DMA((peers,)),
        ],
        cost_estimate=cost(0, 2 * peers * count * rows * LANES * 2),
        name="pack_around",
    )(me, *arrays)


def join(blocks, me):
    peers = len(blocks)

    def body(me_ref, *refs):
        for n in range(peers):
            refs[peers][(me_ref[0] + peers - n) % peers] = refs[n][...]

    return pl.pallas_call(
        body,
        in_specs=[pl.BlockSpec(memory_space=pltpu.SMEM)] + [VMEM] * peers,
        out_specs=VMEM,
        out_shape=jax.ShapeDtypeStruct((peers,) + blocks[0].shape, blocks[0].dtype),
        compiler_params=pltpu.CompilerParams(vmem_limit_bytes=8 << 20),
        cost_estimate=cost(0, 2 << 20),
        name="join",
    )(me, *blocks)


def unpack(grads, chunk, columns, so_far=None):
    peers, count, rows, _ = grads.shape
    given = [] if so_far is None else list(so_far)

    def body(in_ref, *refs):
        outs, sem = refs[len(given):len(given) + count], refs[len(given) + count]
        copies = [
            pltpu.make_async_copy(
                in_ref.at[b, n], outs[n].at[:, pl.ds((chunk * peers + b) * LANES, LANES)], sem.at[b, n])
            for b in range(peers)
            for n in range(count)
        ]
        for copy in copies:
            copy.start()
        for copy in copies:
            copy.wait()

    hbm = pl.BlockSpec(memory_space=pl.ANY)
    return pl.pallas_call(
        body,
        in_specs=[hbm] * (1 + len(given)),
        out_specs=[hbm] * count,
        out_shape=[jax.ShapeDtypeStruct((rows, columns), jnp.bfloat16)] * count,
        scratch_shapes=[pltpu.SemaphoreType.DMA((peers, count))],
        input_output_aliases={1 + n: n for n in range(len(given))},
        compiler_params=pltpu.CompilerParams(vmem_limit_bytes=4 << 20),
        cost_estimate=cost(0, 2 * peers * count * rows * LANES * 2),
        name="unpack",
    )(grads, *given)


def rim_body(info_ref, x_ref, first_ref, second_ref):
    tiles = x_ref.shape[0]
    deep = 2 * REACH
    odd = info_ref[info_ref.shape[0] - 1] > 0.5
    for ref, low in ((first_ref, odd), (second_ref, jnp.logical_not(odd))):
        wide = jnp.where(low, 0, tiles - deep)
        narrow = jnp.where(low, 0, tiles - REACH)
        for t in range(deep):
            ref[t] = x_ref[wide + t, 1]
            ref[deep + t] = x_ref[wide + t, 2]
        for t in range(REACH):
            ref[2 * deep + t] = x_ref[narrow + t, 0]
            ref[2 * deep + REACH + t] = x_ref[narrow + t, 3]


def rims(info, taken):
    shape = jax.ShapeDtypeStruct((6 * REACH,) + taken.shape[2:], taken.dtype)
    return pl.pallas_call(
        rim_body,
        in_specs=[pl.BlockSpec(memory_space=pltpu.SMEM), VMEM],
        out_specs=[VMEM] * 2,
        out_shape=[shape] * 2,
        compiler_params=pltpu.CompilerParams(vmem_limit_bytes=8 << 20),
        cost_estimate=cost(0, 2 << 20),
        name="rims",
    )(info, taken)


def both_heads(block):
    first = lax.broadcasted_iota(jnp.int32, block.shape, 1) < HEAD_DIM
    zero = jnp.zeros_like(block)
    return jnp.concatenate([jnp.where(first, block, zero), jnp.where(first, zero, block)], axis=0)


def score_stage(bias_ref, row, query_tile, grad_tile, key, value, held):
    scores_ref, dprobs_ref, query_ref, grad_ref = held[:4]
    query = both_heads(query_tile * jnp.bfloat16(SCALE))
    grad = both_heads(grad_tile)
    scores = lax.dot_general(key, query, NT, preferred_element_type=jnp.float32)
    for t in range(WINDOW):
        rows = slice(t * TILE, (t + 1) * TILE)
        scores_ref[rows] = scores[rows] + bias_ref[row * WINDOW + t]
    dprobs_ref[...] = lax.dot_general(value, grad, NT, preferred_element_type=jnp.float32)
    query_ref[...] = query
    grad_ref[...] = grad


def softmax_stage(held):
    scores_ref, dprobs_ref, _, _, probs_ref, dscores_ref = held
    parts = [slice(t * TILE, (t + 1) * TILE) for t in range(WINDOW)]
    top = jnp.max(scores_ref[...], axis=0, keepdims=True)
    total = jnp.zeros_like(top)
    for rows in parts:
        weights = jnp.exp(scores_ref[rows] - top)
        scores_ref[rows] = weights
        total += jnp.sum(weights, axis=0, keepdims=True)
    inverse = 1.0 / total
    delta = jnp.zeros_like(top)
    for rows in parts:
        probs = (scores_ref[rows] * inverse).astype(jnp.bfloat16)
        probs_ref[rows] = probs
        delta += jnp.sum(probs.astype(jnp.float32) * dprobs_ref[rows], axis=0, keepdims=True)
    for rows in parts:
        dscores_ref[rows] = (scores_ref[rows] * inverse * (dprobs_ref[rows] - delta)).astype(jnp.bfloat16)


def held_shapes():
    wide, tall = (SPAN, 2 * TILE), (2 * TILE, LANES)
    return [pltpu.VMEM(wide, jnp.float32)] * 2 + [pltpu.VMEM(tall, jnp.bfloat16)] * 2 + [pltpu.VMEM(wide, jnp.bfloat16)] * 2


def query_grad(dscores, key):
    both = lax.dot_general(dscores, key, TN, preferred_element_type=jnp.float32)
    first = lax.broadcasted_iota(jnp.int32, (TILE, LANES), 1) < HEAD_DIM
    return (jnp.where(first, both[:TILE], both[TILE:]) * SCALE).astype(jnp.bfloat16)


def inner_body(ahead, bias_ref, *refs):
    pl.when((bias_ref[bias_ref.shape[0] - 2] > 0.5) == ahead)(lambda: inner_work(bias_ref, *refs))


def inner_work(bias_ref, x_ref, dquery_ref, edge_ref, key_ref, value_ref, *held):
    tiles = x_ref.shape[0]
    held = (held[:6], held[6:])
    for t in range(tiles):
        key_ref[t * TILE:(t + 1) * TILE] = x_ref[t, 1]
        value_ref[t * TILE:(t + 1) * TILE] = x_ref[t, 2]
    edge_ref[...] = jnp.zeros_like(edge_ref)

    def rows_of(n):
        return pl.ds(n * TILE if isinstance(n, int) else pl.multiple_of(n * TILE, TILE), SPAN)

    def begin(n, slot):
        rows = rows_of(n)
        score_stage(
            bias_ref, n + 2 * REACH, x_ref[n + REACH, 0], x_ref[n + REACH, 3], key_ref[rows], value_ref[rows], held[slot])

    def end(n, slot):
        _, _, query_ref, grad_ref, probs_ref, dscores_ref = held[slot]
        rows = rows_of(n)
        dscores = dscores_ref[...]
        edge_ref[0, rows] += jnp.dot(dscores, query_ref[...], preferred_element_type=jnp.float32)
        edge_ref[1, rows] += jnp.dot(probs_ref[...], grad_ref[...], preferred_element_type=jnp.float32)
        dquery_ref[n] = query_grad(dscores, key_ref[rows])

    steps = tiles - 2 * REACH
    begin(0, 0)
    softmax_stage(held[0])
    begin(1, 1)

    def pair(k, _):
        n = 2 * k
        end(n, 0)
        softmax_stage(held[1])
        begin(n + 2, 0)
        end(n + 1, 1)
        softmax_stage(held[0])
        begin(n + 3, 1)
        return 0

    lax.fori_loop(0, steps // 2 - 1, pair, 0)
    end(steps - 2, 0)
    softmax_stage(held[1])
    end(steps - 1, 1)


def inner(bias, taken, ahead):
    tiles = taken.shape[0]
    steps = tiles - 2 * REACH
    whole = tiles * TILE
    return pl.pallas_call(
        functools.partial(inner_body, ahead),
        in_specs=[pl.BlockSpec(memory_space=pltpu.SMEM), VMEM],
        out_specs=[VMEM] * 2,
        out_shape=[
            jax.ShapeDtypeStruct((steps, TILE, LANES), jnp.bfloat16),
            jax.ShapeDtypeStruct((2, whole, LANES), jnp.float32),
        ],
        scratch_shapes=[pltpu.VMEM((whole, LANES), jnp.bfloat16)] * 2 + held_shapes() * 2,
        compiler_params=pltpu.CompilerParams(vmem_limit_bytes=28 << 20),
        cost_estimate=cost(steps * WINDOW * 10 * TILE * TILE * LANES, 5 << 20, steps * WINDOW * 2 * TILE * TILE),
        name="inner",
    )(bias, taken)


def outer_body(
    bias_ref, x_ref, first_ref, second_ref, dquery0_ref, edge0_ref, dquery1_ref, edge1_ref, out_ref, halo_ref, key_ref, value_ref, acc_ref, *held
):
    tiles = x_ref.shape[0]
    deep = 2 * REACH
    held = (held[:6], held[6:])
    odd = bias_ref[bias_ref.shape[0] - 1] > 0.5
    halo_ref[jnp.where(odd, 0, 1)] = first_ref[...]
    halo_ref[jnp.where(odd, 1, 0)] = second_ref[...]
    low_ref, high_ref = halo_ref.at[0], halo_ref.at[1]
    for n, ref in ((1, key_ref), (2, value_ref)):
        for t in range(deep):
            ref[t * TILE:(t + 1) * TILE] = low_ref[(n - 1) * deep + t]
            ref[(deep + t) * TILE:(deep + t + 1) * TILE] = x_ref[t, n]
            ref[(2 * deep + t) * TILE:(2 * deep + t + 1) * TILE] = x_ref[tiles - deep + t, n]
            ref[(3 * deep + t) * TILE:(3 * deep + t + 1) * TILE] = high_ref[(n - 1) * deep + t]
    ahead = bias_ref[bias_ref.shape[0] - 2] > 0.5

    def adopt(dquery_ref, edge_ref):
        acc_ref[...] = edge_ref[...]
        for t in range(tiles - 2 * REACH):
            out_ref[REACH + t, 0] = dquery_ref[t]

    pl.when(ahead)(lambda: adopt(dquery0_ref, edge0_ref))
    pl.when(jnp.logical_not(ahead))(lambda: adopt(dquery1_ref, edge1_ref))

    def place(step):
        j, high = step // 2, step % 2 == 1
        start = j + (2 * deep if high else 0)
        own = (j < REACH) == high
        tile = (tiles - REACH + j if high else j - REACH) if own else None
        return j, high, start, tile

    def begin(step):
        j, high, start, tile = place(step)
        rows = slice(start * TILE, (start + WINDOW) * TILE)
        if tile is not None:
            query_tile, grad_tile = x_ref[tile, 0], x_ref[tile, 3]
        else:
            ref, at = (high_ref, j - REACH) if high else (low_ref, j)
            query_tile, grad_tile = ref[2 * deep + at], ref[2 * deep + REACH + at]
        score_stage(
            bias_ref, j + tiles if high else j, query_tile, grad_tile, key_ref[rows], value_ref[rows], held[step % 2])

    def end(step):
        _, high, start, tile = place(step)
        _, _, query_ref, grad_ref, probs_ref, dscores_ref = held[step % 2]
        low_end, high_end = (2 * deep, 3 * deep) if high else (deep, 2 * deep)
        first, last = max(start, low_end), min(start + WINDOW, high_end)
        part = slice((first - start) * TILE, (last - start) * TILE)
        at = slice((first - deep) * TILE, (last - deep) * TILE)
        acc_ref[0, at] += jnp.dot(dscores_ref[part], query_ref[...], preferred_element_type=jnp.float32)
        acc_ref[1, at] += jnp.dot(probs_ref[part], grad_ref[...], preferred_element_type=jnp.float32)
        if tile is not None:
            out_ref[tile, 0] = query_grad(dscores_ref[...], key_ref[start * TILE:(start + WINDOW) * TILE])

    steps = 2 * deep
    for step in range(steps + 2):
        if step >= 2:
            end(step - 2)
        if 1 <= step <= steps:
            softmax_stage(held[(step - 1) % 2])
        if step < steps:
            begin(step)
    for n in range(2):
        for t in range(2 * deep):
            tile = t if t < deep else tiles - 2 * deep + t
            out_ref[tile, 1 + n] = acc_ref[n, t * TILE:(t + 1) * TILE].astype(jnp.bfloat16)


def outer(bias, taken, first, second, *parts):
    tiles = taken.shape[0]
    steps = 4 * REACH
    return pl.pallas_call(
        outer_body,
        in_specs=[pl.BlockSpec(memory_space=pltpu.SMEM)] + [VMEM] * 7,
        out_specs=VMEM,
        out_shape=jax.ShapeDtypeStruct((tiles, 3, TILE, LANES), jnp.bfloat16),
        scratch_shapes=[pltpu.VMEM((2,) + first.shape, jnp.bfloat16)]
        + [pltpu.VMEM((8 * REACH * TILE, LANES), jnp.bfloat16)] * 2
        + [pltpu.VMEM(parts[1].shape, jnp.float32)]
        + held_shapes() * 2,
        compiler_params=pltpu.CompilerParams(vmem_limit_bytes=28 << 20),
        cost_estimate=cost(steps * WINDOW * 8 * TILE * TILE * LANES, 6 << 20, steps * WINDOW * 2 * TILE * TILE),
        name="outer",
    )(bias, taken, first, second, *parts)


def tile_bias(near_mask, motion_count, first, tiles):
    total = near_mask.shape[0]
    near = lax.dynamic_slice_in_dim(jnp.pad(near_mask, ((REACH, REACH), (0, 0))), first, tiles + 2 * REACH, 0) == 1
    far = lax.dynamic_slice_in_dim(jnp.pad(motion_count, (REACH, REACH)), first, tiles + 2 * REACH, 0) >= 2
    own = jnp.ones_like(far)
    allowed = jnp.stack([far, near[:, 0], own, near[:, 1], far], axis=1)
    index = first - REACH + jnp.arange(tiles + 2 * REACH)
    others = index[:, None] + jnp.arange(-REACH, REACH + 1)[None, :]
    allowed &= (others >= 0) & (others < total)
    group = first // tiles
    ahead = ((group > 0) & (group % LAUNCH == 0)).astype(jnp.float32)
    odd = (group % 2).astype(jnp.float32)
    return jnp.concatenate([jnp.where(allowed, 0.0, -1e30).astype(jnp.float32).reshape(-1), ahead[None], odd[None]])


def gate(table):
    def body(in_ref, out_ref):
        out_ref[...] = in_ref[...]

    return pl.pallas_call(
        body,
        in_specs=[VMEM],
        out_specs=VMEM,
        out_shape=jax.ShapeDtypeStruct(table.shape, table.dtype),
        compiler_params=pltpu.CompilerParams(vmem_limit_bytes=1 << 20),
        cost_estimate=cost(0, 1 << 10),
        name="gate",
    )(table)


def per_device(query_states, key_states, value_states, output_grad, near_mask, motion_count):
    tiles, groups = lax.axis_size("blk"), lax.axis_size("seq")
    columns = query_states.shape[1]
    arrays = (query_states, key_states, value_states, output_grad)

    def exchange(x):
        return lax.all_to_all(x, "blk", split_axis=0, concat_axis=0, tiled=True)

    def swap(x, parity):
        right = [(i, i + 1) for i in range(groups - 1) if i % 2 == parity]
        return lax.ppermute(x, "seq", right + [(j, i) for i, j in right])

    taken, results = [], None
    bias = tile_bias(near_mask, motion_count, lax.axis_index("seq") * tiles, tiles)
    me = lax.axis_index("blk").reshape(1)
    packed = pack(arrays, 0, tiles)
    taken.append(exchange(packed))
    blocks = list(pack_around(arrays, 1, tiles, me))
    for n in ORDER:
        blocks[n] = lax.ppermute(blocks[n], "blk", [(i, (i + n) % tiles) for i in range(tiles)])
    taken.append(join(blocks, me))
    info = gate(bias)
    for c in range(CHUNKS):
        first, second = rims(info, taken[c])
        parts = inner(info, taken[c], True)
        second = swap(second, 1)
        first = swap(first, 0)
        parts += inner(info, taken[c], False)
        out = outer(info, taken[c], first, second, *parts)
        back = exchange(out)
        results = unpack(back, c, columns, results)
    return tuple(results)


def solution(mesh):
    spec = P(("seq", "blk"), None)
    return jax.shard_map(
        per_device, mesh=mesh, in_specs=(spec,) * 4 + (P(), P()), out_specs=(spec,) * 3, check_vma=False
    )
```
